32 devices in a mesh: freq: 4 (over y, x), panel: 8 (over z, core).
Axes of the slice: x: 2, y: 2, z: 4, core: 2. Of those that a mesh axis runs over, the one named last changes fastest.
Arguments:
- fields: bfloat16 [128, 16, 16384], P('freq', None, 'panel'), may hold values from -6 to 6
- quad_index: int32 [16384], P('panel'), may hold values from 0 to 5
- band_width: int32 [128], P('freq'), may hold values from 1 to 64, as said below
Outputs:
- pair_blocks: float32 [128, 16384], P('freq', 'panel')
The draws below stay inside these ranges and needn't reach their ends.
Inputs may be any that keep to these rules, and one draw needn't show every extreme that they name: `band_width`: some frequency has band width exactly 64.
All inputs are finite; a program needn't handle non-finite values.
Results may differ from the reference program's by a relative error of at most 0.0029.
Values may be sent and summed in bfloat16 or wider, within the bound.
A program may use at most 128 MiB of HBM per device.

```python
import math
import jax
import jax.numpy as jnp
from jax import lax

COMP = 16
FREQS = 128
PANELS = 16384
BAND = 64


def draw_band_width(key, part):
    first_key, second_key = jax.random.split(key)
    widths = jax.random.randint(first_key, (FREQS,), 1, BAND + 1)
    widest = jax.random.randint(second_key, (), 0, FREQS)
    return jnp.where(jnp.arange(FREQS) == widest, BAND, widths).astype(jnp.int32)


def plant(values, rng, smallest, largest):
    longest = values.shape.index(max(values.shape))
    spots = []
    for shift in (0, 1):
        where = [jax.random.randint(jax.random.fold_in(rng, axis), (), 0, length) for axis, length in enumerate(values.shape)]
        where[longest] = (where[longest] + shift) % values.shape[longest]
        spots.append(tuple(where))
    return values.at[spots[0]].set(smallest).at[spots[1]].set(largest)


def level_of(rng, extent, cuts, least, high):
    factor_of = 1.0
    for dim, parts in cuts:
        draws = jax.random.uniform(jax.random.fold_in(jax.random.fold_in(rng, 6), dim), (parts,), jnp.float32, least / len(cuts), high / len(cuts))
        factor_of = factor_of * jnp.repeat(jnp.exp(draws), extent[dim] // parts).reshape((-1,) + (1,) * (len(extent) - 1 - dim))
    return factor_of


def bell_draw(key, extent, scale, bound, cuts=(), kind=jnp.bfloat16):
    entries = scale * jax.random.normal(key, extent, jnp.float32)
    if cuts:
        entries = entries * level_of(key, extent, cuts, -0.22, 0.18)
    return jnp.clip(entries, -bound, bound).astype(kind)


def setup_inputs(seed: int = 0) -> dict:
    keys = jax.random.split(jax.random.key(seed), 4)
    fields = bell_draw(keys[0], (FREQS, COMP, PANELS), 1.0, 6.0, ((0, 4), (2, 8)))
    quad_index = plant(jax.random.randint(keys[1], (PANELS,), 0, 6), jax.random.fold_in(keys[1], 1), 0, 5).astype(jnp.int32)
    band_width = draw_band_width(jax.random.fold_in(keys[3], 71), 0)
    return {"fields": fields, "quad_index": quad_index, "band_width": band_width}


QUAD_TABLE = (0.2, 0.45, 0.8, 1.1, 1.6, 2.3)

def reference(fields, quad_index, band_width):
    weight = jnp.asarray(QUAD_TABLE, jnp.float32)[quad_index]
    padded = jnp.concatenate([fields, jnp.zeros((BAND, COMP, PANELS), jnp.bfloat16)], 0)
    offsets = jnp.arange(BAND, dtype=jnp.int32) + 1

    def one_row(index):
        own = lax.dynamic_index_in_dim(fields, index, 0, keepdims=False)
        own_scaled = (own.astype(jnp.float32) * weight).astype(jnp.bfloat16)
        partner = lax.dynamic_slice_in_dim(padded, index + 1, BAND, 0).reshape(BAND * COMP, PANELS)
        gram = lax.dot_general(own_scaled, partner, (((1,), (1,)), ((), ())), preferred_element_type=jnp.float32)
        gram = gram.reshape(COMP, BAND, COMP).transpose(1, 0, 2)
        live = offsets <= band_width[index]
        return jnp.where(live[:, None, None], gram, jnp.float32(0.0)).reshape(BAND * COMP * COMP)
    rows = lax.map(one_row, jnp.arange(FREQS, dtype=jnp.int32))
    return rows * jnp.float32(1.0 / math.sqrt(PANELS))
```

```python
import functools
import math

import jax
import jax.numpy as jnp
from jax import lax
from jax.experimental import pallas as pl
from jax.experimental.pallas import tpu as pltpu
from jax.sharding import PartitionSpec as P

COMP = 16
REACH = 2
LANES = 128
CORES = 2
MESH = pl.DeviceIdType.MESH

QUAD_TABLE = (0.2, 0.45, 0.8, 1.1, 1.6, 2.3)


def shifted(x, axis, by):
    devices = lax.axis_size(axis)
    pairs = [(i, i + by) for i in range(devices) if 0 <= i + by < devices]
    return lax.ppermute(x, axis, pairs)


def plain(fields, quad_index, band_width):
    freq_local = fields.shape[0]
    panel_local = fields.shape[2]
    band = REACH * freq_local
    table = jnp.asarray(QUAD_TABLE, jnp.float32)
    matches = quad_index[None, :] == jnp.arange(6, dtype=jnp.int32)[:, None]
    weight = jnp.sum(jnp.where(matches, table[:, None], jnp.float32(0.0)), 0)
    scaled = (fields.astype(jnp.float32) * weight).astype(jnp.bfloat16)
    own_rows = scaled.reshape(freq_local * COMP, panel_local)
    partners = [fields]
    for distance in range(1, REACH + 1):
        partners.append(shifted(fields, "freq", -distance))
    grams = []
    for partner in partners:
        grams.append(
            lax.dot_general(
                own_rows,
                partner.reshape(freq_local * COMP, panel_local),
                (((1,), (1,)), ((), ())),
                preferred_element_type=jnp.float32,
            )
        )
    stacked = jnp.concatenate(grams, 1).reshape(freq_local, COMP, (REACH + 1) * freq_local, COMP)

    def pick_band(block, row_index):
        return lax.dynamic_slice_in_dim(block, row_index + 1, band, 1)

    picked = jax.vmap(pick_band)(stacked, jnp.arange(freq_local, dtype=jnp.int32))
    picked = picked.transpose(0, 2, 1, 3)
    offsets = jnp.arange(band, dtype=jnp.int32) + 1
    live_mask = offsets[None, :] <= band_width[:, None]
    picked = jnp.where(live_mask[:, :, None, None], picked, jnp.float32(0.0))
    panels_total = panel_local * lax.axis_size("panel")
    terms = picked.reshape(freq_local, band * COMP * COMP) * jnp.float32(
        1.0 / math.sqrt(panels_total)
    )
    return lax.psum_scatter(terms, "panel", scatter_dimension=1, tiled=True)


OWN, XG, DG = 0, 1, 2


def kernel(
    nf, npan, f_hbm, q_ref, bw_ref, out_ref,
    own, scaled, xbuf, ubuf, dbuf, xs, ds, acc, keep, away, cxin, zout, zin, total, fwd, fin,
    local_sem, fsend, frecv, csend, crecv, zsend, zrecv, gsend, grecv,
):
    rows, panels = own.shape
    half = panels // 2
    block = rows
    freqs = rows // COMP
    oct_rows = 8 * COMP
    octs = rows // oct_rows
    nz = npan // CORES
    f32, bf16 = jnp.float32, jnp.bfloat16

    f = lax.axis_index("freq")
    p = lax.axis_index("panel")
    z, core = p // CORES, lax.rem(p, CORES)
    odd = lax.rem(f, 2)
    mate = f + 1 - 2 * odd
    has_u = f + 2 < nf
    has_d = f >= 2
    has_x = jnp.logical_or(odd == 1, has_u)
    partner = p + 1 - 2 * core

    def dev(ff, pp):
        return {"freq": ff, "panel": pp}

    load = pltpu.make_async_copy(f_hbm, own, local_sem)
    load.start()

    barrier = pltpu.get_barrier_semaphore()

    def greet(ff, pp):
        pl.semaphore_signal(barrier, inc=1, device_id=dev(ff, pp), device_id_type=MESH)

    greet(mate, p)
    greet(f, partner)
    for zd in range(nz):
        @pl.when(z != zd)
        def _(zd=zd):
            greet(f, zd * CORES + core)

    @pl.when(has_u)
    def _():
        greet(f + 2, p)

    @pl.when(has_d)
    def _():
        greet(f - 2, p)

    count = 1 + nz + jnp.where(has_u, 1, 0) + jnp.where(has_d, 1, 0)
    pl.semaphore_wait(barrier, count)

    def half_at(which):
        return pl.ds(pl.multiple_of(which * half, LANES), half)

    def field_copy(which, dst, slot, ff):
        return pltpu.make_async_remote_copy(
            src_ref=f_hbm.at[:, half_at(which)], dst_ref=dst,
            send_sem=fsend.at[slot], recv_sem=frecv.at[slot],
            device_id=dev(ff, p), device_id_type=MESH,
        )

    to_mate = field_copy(1 - odd, xbuf, 0, mate)
    to_lower = field_copy(0, ubuf, 1, f - 2)
    to_upper = field_copy(1, dbuf, 2, f + 2)
    to_mate.start()

    @pl.when(has_d)
    def _():
        to_lower.start()

    @pl.when(has_u)
    def _():
        to_upper.start()

    def weight_at(where):
        index = q_ref[:, where]
        w = jnp.zeros(index.shape, f32)
        for value, entry in enumerate(QUAD_TABLE):
            w = jnp.where(index == value, jnp.float32(entry), w)
        return w

    def scale(src, dst, where):
        w = weight_at(where)

        def step(i, carry):
            at = pl.ds(pl.multiple_of(i * 32, 32), 32)
            dst[at, :] = (src[at, :].astype(f32) * w).astype(bf16)
            return carry

        lax.fori_loop(0, rows // 32, step, 0)

    def gram(left, left_at, right, right_at, slot, rel):
        tall = min(256, rows)

        def step(i, carry):
            at = pl.ds(pl.multiple_of(i * tall, tall), tall)
            acc[slot, at, rel * block:(rel + 1) * block] = lax.dot_general(
                left[at, left_at], right[:, right_at],
                (((1,), (1,)), ((), ())), preferred_element_type=f32,
            )
            return carry

        lax.fori_loop(0, rows // tall, step, 0)

    def clear(slot, rel):
        acc[slot, :, rel * block:(rel + 1) * block] = jnp.zeros((rows, block), f32)

    clear(XG, 0)
    clear(XG, 2)
    clear(DG, 0)

    @pl.when(odd == 0)
    def _():
        clear(DG, 1)

    @pl.when(odd == 1)
    def _():
        clear(OWN, 1)

    @pl.when(jnp.logical_not(has_u))
    def _():
        clear(OWN, 2)

    load.wait()
    everything = pl.ds(0, panels)
    first = pl.ds(0, half)
    second = pl.ds(half, half)
    scale(own, scaled, everything)
    gram(scaled, everything, own, everything, OWN, 0)

    to_mate.wait_recv()
    scale(xbuf, xs, half_at(odd))

    @pl.when(odd == 0)
    def _():
        gram(scaled, first, xbuf, first, OWN, 1)

    @pl.when(odd == 1)
    def _():
        gram(xs, first, own, second, XG, 1)

    @pl.when(has_u)
    def _():
        to_lower.wait_recv()
        gram(scaled, first, ubuf, first, OWN, 2)

        @pl.when(odd == 0)
        def _():
            gram(xs, first, ubuf, first, XG, 1)

    @pl.when(has_d)
    def _():
        to_upper.wait_recv()
        scale(dbuf, ds, second)
        gram(ds, first, own, second, DG, 2)

        @pl.when(odd == 1)
        def _():
            gram(ds, first, xbuf, first, DG, 1)

    def span(slot, zd):
        lo_k, hi_k = zd * CORES, zd * CORES + CORES - 1
        if slot == OWN:
            return 0, octs
        lo = max(0, octs - 1 - hi_k)
        hi = min(octs - 1, 2 * octs - 1 - lo_k) if slot == XG else octs - 1
        return lo, hi + 1

    def tiles(slot, which, dst):
        for zd in range(nz):
            lo, hi = span(slot, zd)

            def step(o, carry, zd=zd):
                lane = pl.multiple_of((o + zd * CORES + which) * LANES, LANES)
                for c in range(8):
                    at = pl.ds(pl.multiple_of(o * oct_rows + c * COMP, COMP), COMP)
                    if c == 7:
                        lane_next = pl.multiple_of(lane + LANES, LANES)
                        value = acc[slot, at, pl.ds(lane_next, LANES)]
                    else:
                        pair = acc[slot, at, pl.ds(lane, 2 * LANES)]
                        value = pltpu.roll(pair, 2 * LANES - COMP * (c + 1), 1)[:, :LANES]
                    dst[slot, zd, at, :] = value.astype(dst.dtype)
                return carry

            lax.fori_loop(lo, hi, step, 0)

    def core_copy(slot, zd):
        lo, hi = span(slot, zd)
        at = pl.ds(lo * oct_rows, (hi - lo) * oct_rows)
        return pltpu.make_async_remote_copy(
            src_ref=away.at[slot, zd, at, :], dst_ref=cxin.at[slot, zd, at, :],
            send_sem=csend.at[slot, zd], recv_sem=crecv.at[slot, zd],
            device_id=dev(f, partner), device_id_type=MESH,
        )

    def z_copy(slot, zd, source):
        lo, hi = span(slot, zd)
        at = pl.ds(lo * oct_rows, (hi - lo) * oct_rows)
        return pltpu.make_async_remote_copy(
            src_ref=zout.at[slot, zd, at, :], dst_ref=zin.at[slot, source, at, :],
            send_sem=zsend.at[slot, zd], recv_sem=zrecv.at[slot, source],
            device_id=dev(f, zd * CORES + core), device_id_type=MESH,
        )

    def emit(slot):
        tiles(slot, 1 - core, away)
        for zd in range(nz):
            core_copy(slot, zd).start()
        tiles(slot, core, keep)

    def relay(slot):
        for zd in range(nz):
            core_copy(slot, zd).wait_recv()
            lo, hi = span(slot, zd)

            def step(o, carry, zd=zd):
                at = pl.ds(pl.multiple_of(o * oct_rows, oct_rows), oct_rows)
                both = keep[slot, zd, at, :] + cxin[slot, zd, at, :].astype(f32)

                @pl.when(z == zd)
                def _():
                    total[slot, at, :] = both

                @pl.when(z != zd)
                def _():
                    zout[slot, zd, at, :] = both.astype(bf16)

                return carry

            lax.fori_loop(lo, hi, step, 0)

            @pl.when(z != zd)
            def _(zd=zd):
                z_copy(slot, zd, z).start()

    def gather(slot):
        for zd in range(nz):
            lo, hi = span(slot, zd)

            @pl.when(z == zd)
            def _(zd=zd, lo=lo, hi=hi):
                for source in range(nz):
                    if source == zd:
                        continue
                    z_copy(slot, zd, source).wait_recv()

                def step(o, carry):
                    at = pl.ds(pl.multiple_of(o * oct_rows, oct_rows), oct_rows)
                    value = total[slot, at, :]
                    for source in range(nz):
                        if source != zd:
                            value = value + zin[slot, source, at, :].astype(f32)
                    total[slot, at, :] = value
                    return carry

                lax.fori_loop(lo, hi, step, 0)

    def drain(slot):
        for zd in range(nz):
            core_copy(slot, zd).wait_send()

            @pl.when(z != zd)
            def _(zd=zd):
                z_copy(slot, zd, z).wait_send()

    def forward(slot, ff):
        return pltpu.make_async_remote_copy(
            src_ref=total.at[slot], dst_ref=fwd.at[slot],
            send_sem=gsend.at[slot], recv_sem=grecv.at[slot],
            device_id=dev(ff, p), device_id_type=MESH,
        )

    present = {OWN: None, XG: has_x, DG: has_d}

    def each(order, act):
        for slot in order:
            if present[slot] is None:
                act(slot)
            else:
                pl.when(present[slot])(functools.partial(act, slot))

    total[XG] = jnp.zeros(total.shape[1:], f32)
    total[DG] = jnp.zeros(total.shape[1:], f32)
    order = (XG, DG, OWN)
    each(order, emit)
    each(order, relay)
    give_x = forward(XG, mate)
    give_d = forward(DG, f - 2)

    @pl.when(has_x)
    def _():
        gather(XG)
        give_x.start()

    @pl.when(has_d)
    def _():
        gather(DG)
        give_d.start()

    gather(OWN)
    mate_gives = jnp.logical_or(odd == 0, f + 1 < nf)

    def take(slot):
        def step(o, carry):
            at = pl.ds(pl.multiple_of(o * oct_rows, oct_rows), oct_rows)
            total[OWN, at, :] = total[OWN, at, :] + fwd[slot, at, :]
            return carry

        lax.fori_loop(0, octs, step, 0)

    @pl.when(mate_gives)
    def _():
        give_x.wait_recv()
        take(XG)

    @pl.when(has_u)
    def _():
        give_d.wait_recv()
        take(DG)

    fin[...] = total[OWN]
    eye = lax.broadcasted_iota(jnp.int32, (freqs, freqs), 0) == lax.broadcasted_iota(
        jnp.int32, (freqs, freqs), 1
    )
    width = jnp.sum(
        jnp.where(eye, jnp.broadcast_to(bw_ref[...].astype(f32), (freqs, freqs)), 0.0), 1, keepdims=True
    )
    width = jnp.broadcast_to(width, (freqs, LANES))
    norm = jnp.float32(1.0 / math.sqrt(panels * npan))
    part = lax.broadcasted_iota(jnp.int32, (freqs, LANES), 1) // COMP
    for h in range(COMP // 8):
        values = [fin[pl.ds(h * 8 + a, freqs, stride=COMP), :] for a in range(8)]
        for bit in (1, 2, 4):
            upper = lax.rem(part // bit, 2) == 1
            fresh = list(values)
            for i in range(8):
                if i & bit:
                    continue
                j = i | bit
                fresh[i] = jnp.where(upper, pltpu.roll(values[j], COMP * bit, 1), values[i])
                fresh[j] = jnp.where(upper, values[j], pltpu.roll(values[i], LANES - COMP * bit, 1))
            values = fresh
        for k in range(8):
            offset = (p * 8 + k + 1).astype(f32)
            live = offset <= width
            start = (k * (COMP // 8) + h) * LANES
            out_ref[:, start:start + LANES] = jnp.where(live, values[k] * norm, 0.0)

    to_mate.wait_send()

    @pl.when(has_d)
    def _():
        to_lower.wait_send()
        give_d.wait_send()

    @pl.when(has_u)
    def _():
        to_upper.wait_send()

    @pl.when(has_x)
    def _():
        give_x.wait_send()

    each(order, drain)


def fused(nf, npan, fields, quad_index, band_width):
    freqs, comp, panels = fields.shape
    rows = freqs * comp
    nz = npan // CORES
    half = panels // 2
    out_cols = REACH * freqs * comp * comp // npan
    bf16, f32 = jnp.bfloat16, jnp.float32
    dma = pltpu.SemaphoreType.DMA
    vmem = pl.BlockSpec(memory_space=pltpu.VMEM)
    return pl.pallas_call(
        functools.partial(kernel, nf, npan),
        out_shape=jax.ShapeDtypeStruct((freqs, out_cols), f32),
        in_specs=[pl.BlockSpec(memory_space=pl.ANY), vmem, vmem],
        out_specs=vmem,
        scratch_shapes=[
            pltpu.VMEM((rows, panels), bf16),
            pltpu.VMEM((rows, panels), bf16),
            pltpu.VMEM((rows, half), bf16),
            pltpu.VMEM((rows, half), bf16),
            pltpu.VMEM((rows, half), bf16),
            pltpu.VMEM((rows, half), bf16),
            pltpu.VMEM((rows, half), bf16),
            pltpu.VMEM((3, rows, (REACH + 1) * rows), f32),
            pltpu.VMEM((3, nz, rows, LANES), f32),
            pltpu.VMEM((3, nz, rows, LANES), bf16),
            pltpu.VMEM((3, nz, rows, LANES), bf16),
            pltpu.VMEM((3, nz, rows, LANES), bf16),
            pltpu.VMEM((3, nz, rows, LANES), bf16),
            pltpu.VMEM((3, rows, LANES), f32),
            pltpu.VMEM((3, rows, LANES), f32),
            pltpu.VMEM((rows, LANES), f32),
            dma,
            dma((3,)), dma((3,)),
            dma((3, nz)), dma((3, nz)),
            dma((3, nz)), dma((3, nz)),
            dma((3,)), dma((3,)),
        ],
        compiler_params=pltpu.CompilerParams(
            collective_id=0, has_side_effects=True, vmem_limit_bytes=58 * 1024 * 1024
        ),
    )(fields.reshape(rows, panels), quad_index.reshape(1, panels), band_width.reshape(1, freqs))


def local(nf, npan, fields, quad_index, band_width):
    freqs, comp, panels = fields.shape
    share = REACH * freqs * comp // npan
    fits = nf % 2 == 0 and npan % CORES == 0 and share == LANES and freqs % 8 == 0 and panels % (4 * LANES) == 0
    if not fits:
        return plain(fields, quad_index, band_width)
    return fused(nf, npan, fields, quad_index, band_width)


def solution(mesh):
    placed = (P("freq", None, "panel"), P("panel"), P("freq"))
    return jax.shard_map(
        functools.partial(local, mesh.shape["freq"], mesh.shape["panel"]),
        mesh=mesh, in_specs=placed, out_specs=P("freq", "panel"), check_vma=False,
    )
```

```python
import functools
import math

import jax
import jax.numpy as jnp
from jax import lax
from jax.experimental import pallas as pl
from jax.experimental.pallas import tpu as pltpu
from jax.sharding import PartitionSpec as P

COMP = 16
REACH = 2
LANES = 128
CORES = 2
MESH = pl.DeviceIdType.MESH

QUAD_TABLE = (0.2, 0.45, 0.8, 1.1, 1.6, 2.3)


def shifted(x, axis, by):
    devices = lax.axis_size(axis)
    pairs = [(i, i + by) for i in range(devices) if 0 <= i + by < devices]
    return lax.ppermute(x, axis, pairs)


def plain(fields, quad_index, band_width):
    freq_local = fields.shape[0]
    panel_local = fields.shape[2]
    band = REACH * freq_local
    table = jnp.asarray(QUAD_TABLE, jnp.float32)
    matches = quad_index[None, :] == jnp.arange(6, dtype=jnp.int32)[:, None]
    weight = jnp.sum(jnp.where(matches, table[:, None], jnp.float32(0.0)), 0)
    scaled = (fields.astype(jnp.float32) * weight).astype(jnp.bfloat16)
    own_rows = scaled.reshape(freq_local * COMP, panel_local)
    partners = [fields]
    for distance in range(1, REACH + 1):
        partners.append(shifted(fields, "freq", -distance))
    grams = []
    for partner in partners:
        grams.append(
            lax.dot_general(
                own_rows,
                partner.reshape(freq_local * COMP, panel_local),
                (((1,), (1,)), ((), ())),
                preferred_element_type=jnp.float32,
            )
        )
    stacked = jnp.concatenate(grams, 1).reshape(freq_local, COMP, (REACH + 1) * freq_local, COMP)

    def pick_band(block, row_index):
        return lax.dynamic_slice_in_dim(block, row_index + 1, band, 1)

    picked = jax.vmap(pick_band)(stacked, jnp.arange(freq_local, dtype=jnp.int32))
    picked = picked.transpose(0, 2, 1, 3)
    offsets = jnp.arange(band, dtype=jnp.int32) + 1
    live_mask = offsets[None, :] <= band_width[:, None]
    picked = jnp.where(live_mask[:, :, None, None], picked, jnp.float32(0.0))
    panels_total = panel_local * lax.axis_size("panel")
    terms = picked.reshape(freq_local, band * COMP * COMP) * jnp.float32(
        1.0 / math.sqrt(panels_total)
    )
    return lax.psum_scatter(terms, "panel", scatter_dimension=1, tiled=True)


OWN, XG, DG = 0, 1, 2


def kernel(
    nf, npan, f_hbm, q_ref, bw_ref, out_ref,
    own, scaled, xbuf, ubuf, dbuf, xs, ds, acc, keep, away, cxin, zout, zin, total, fwd, fin,
    local_sem, fsend, frecv, csend, crecv, zsend, zrecv, gsend, grecv,
):
    rows, panels = own.shape
    half = panels // 2
    block = rows
    freqs = rows // COMP
    oct_rows = 8 * COMP
    octs = rows // oct_rows
    nz = npan // CORES
    f32, bf16 = jnp.float32, jnp.bfloat16

    f = lax.axis_index("freq")
    p = lax.axis_index("panel")
    z, core = p // CORES, lax.rem(p, CORES)
    odd = lax.rem(f, 2)
    mate = f + 1 - 2 * odd
    has_u = f + 2 < nf
    has_d = f >= 2
    has_x = jnp.logical_or(odd == 1, has_u)
    partner = p + 1 - 2 * core

    def dev(ff, pp):
        return {"freq": ff, "panel": pp}

    load = pltpu.make_async_copy(f_hbm, own, local_sem)
    load.start()

    barrier = pltpu.get_barrier_semaphore()

    def greet(ff, pp):
        pl.semaphore_signal(barrier, inc=1, device_id=dev(ff, pp), device_id_type=MESH)

    greet(mate, p)
    greet(f, partner)
    for zd in range(nz):
        @pl.when(z != zd)
        def _(zd=zd):
            greet(f, zd * CORES + core)

    @pl.when(has_u)
    def _():
        greet(f + 2, p)

    @pl.when(has_d)
    def _():
        greet(f - 2, p)

    count = 1 + nz + jnp.where(has_u, 1, 0) + jnp.where(has_d, 1, 0)
    pl.semaphore_wait(barrier, count)

    def half_at(which):
        return pl.ds(pl.multiple_of(which * half, LANES), half)

    def rows_of(o, n=1):
        return pl.ds(pl.multiple_of(o * oct_rows, oct_rows), n * oct_rows)

    def field_copy(which, dst, slot, ff, o):
        return pltpu.make_async_remote_copy(
            src_ref=f_hbm.at[rows_of(o), half_at(which)], dst_ref=dst.at[rows_of(o), :],
            send_sem=fsend.at[slot, o], recv_sem=frecv.at[slot, o],
            device_id=dev(ff, p), device_id_type=MESH,
        )

    def to_mate(o):
        return field_copy(1 - odd, xbuf, 0, mate, o)

    def to_lower(o):
        return field_copy(0, ubuf, 1, f - 2, o)

    def to_upper(o):
        return field_copy(1, dbuf, 2, f + 2, o)

    for o in range(octs):
        to_mate(o).start()

        @pl.when(has_d)
        def _(o=o):
            to_lower(o).start()

        @pl.when(has_u)
        def _(o=o):
            to_upper(o).start()

    def weight_at(where):
        index = q_ref[:, where]
        w = jnp.zeros(index.shape, f32)
        for value, entry in enumerate(QUAD_TABLE):
            w = jnp.where(index == value, jnp.float32(entry), w)
        return w

    def scale(src, dst, where, o, n):
        w = weight_at(where)

        def step(i, carry):
            at = pl.ds(pl.multiple_of(o * oct_rows + i * 32, 32), 32)
            dst[at, :] = (src[at, :].astype(f32) * w).astype(bf16)
            return carry

        lax.fori_loop(0, n * oct_rows // 32, step, 0)

    def gram(left, left_at, lo, n, right, right_at, ro, m, slot, rel):
        tall = 2 if n % 2 == 0 else 1
        first_col = rel * block + ro * oct_rows

        def step(i, carry):
            at = rows_of(lo + i * tall, tall)
            acc[slot, at, first_col:first_col + m * oct_rows] = lax.dot_general(
                left[at, left_at], right[ro * oct_rows:(ro + m) * oct_rows, right_at],
                (((1,), (1,)), ((), ())), preferred_element_type=f32,
            )
            return carry

        if n == tall:
            step(0, 0)
        else:
            lax.fori_loop(0, n // tall, step, 0)

    def clear(slot, tile):
        acc[slot, :, tile * LANES:(tile + 1) * LANES] = jnp.zeros((rows, LANES), f32)

    clear(XG, octs - 1)
    clear(XG, 2 * octs)
    clear(DG, octs - 1)

    @pl.when(odd == 0)
    def _():
        clear(DG, 2 * octs - 1)

    @pl.when(odd == 1)
    def _():
        clear(OWN, octs)
        clear(OWN, 2 * octs - 1)

    @pl.when(jnp.logical_not(has_u))
    def _():
        clear(OWN, 2 * octs)

    def valid(slot, o, pp):
        t = o + pp
        low, high = t >= octs - 1, t <= 2 * octs - 1
        if slot == OWN:
            return jnp.logical_or(
                t <= octs - 1,
                jnp.logical_or(
                    jnp.logical_and(odd == 0, high),
                    jnp.logical_and(has_u, t >= 2 * octs - 1),
                ),
            )
        if slot == XG:
            return jnp.logical_and(has_x, jnp.logical_and(low, high))
        upper = jnp.logical_or(t >= 2 * octs - 1, jnp.logical_and(odd == 1, low))
        return jnp.logical_and(has_d, upper)

    def core_copy(slot, o, pp):
        zd = pp // CORES
        return pltpu.make_async_remote_copy(
            src_ref=away.at[slot, pp, rows_of(o), :], dst_ref=cxin.at[slot, zd, rows_of(o), :],
            send_sem=csend.at[slot, zd, o], recv_sem=crecv.at[slot, zd, o],
            device_id=dev(f, partner), device_id_type=MESH,
        )

    def z_copy(slot, o, zd, source):
        return pltpu.make_async_remote_copy(
            src_ref=zout.at[slot, zd, rows_of(o), :], dst_ref=zin.at[slot, source, rows_of(o), :],
            send_sem=zsend.at[slot, zd, o], recv_sem=zrecv.at[slot, source, o],
            device_id=dev(f, zd * CORES + core), device_id_type=MESH,
        )

    def walk(act, slot, o, t, n, do, dt):
        def step(i, carry):
            oo, tt = o + i * do, t + i * dt
            act(slot, oo, tt - oo, tt)
            return carry

        if n > 0:
            lax.fori_loop(0, n, step, 0)

    def make(slot, o, pp, t):
        lane = pl.multiple_of(t * LANES, LANES)
        for c in range(8):
            at = pl.ds(pl.multiple_of(o * oct_rows + c * COMP, COMP), COMP)
            if c == 7:
                value = acc[slot, at, pl.ds(pl.multiple_of(lane + LANES, LANES), LANES)]
            else:
                pair = acc[slot, at, pl.ds(lane, 2 * LANES)]
                value = pltpu.roll(pair, 2 * LANES - COMP * (c + 1), 1)[:, :LANES]
            keep[slot, pp, at, :] = value
            away[slot, pp, at, :] = value.astype(bf16)

        @pl.when(lax.rem(pp, CORES) != core)
        def _():
            core_copy(slot, o, pp).start()

    def join(slot, o, pp, t):
        @pl.when(lax.rem(pp, CORES) == core)
        def _():
            zd = pp // CORES
            core_copy(slot, o, pp).wait_recv()
            both = keep[slot, pp, rows_of(o), :] + cxin[slot, zd, rows_of(o), :].astype(f32)

            @pl.when(z == zd)
            def _():
                total[slot, rows_of(o), :] = both

            @pl.when(z != zd)
            def _():
                zout[slot, zd, rows_of(o), :] = both.astype(bf16)
                z_copy(slot, o, zd, z).start()

    def both_ways(jobs):
        for act in (make, join):
            for job in jobs:
                if len(job) == 2:
                    @pl.when(job[0])
                    def _(job=job, act=act):
                        for inner in job[1]:
                            walk(act, *inner)
                else:
                    walk(act, *job)

    load.wait()
    everything = pl.ds(0, panels)
    first = pl.ds(0, half)
    second = pl.ds(half, half)
    even_now, odd_now = odd == 0, odd == 1
    scale(own, scaled, everything, 0, octs)
    gram(scaled, everything, 0, octs, own, everything, 0, octs, OWN, 0)
    jobs = [(OWN, 0, t, t + 1, 1, 0) for t in range(octs - 1)]
    jobs.append((odd_now, [(OWN, 0, octs - 1, octs, 1, 0)]))
    both_ways(jobs)

    def corner(slot, i):
        last = i == octs - 1
        out = [(slot, i, octs - 1, i + 1 + last, 0, 1), (slot, 0, octs - 1 + i, i, 1, 0)]
        if last:
            out.append((slot, 0, 2 * octs - 1, i, 1, 0))
        return out

    for i in range(octs):
        last = i == octs - 1
        to_mate(i).wait_recv()
        scale(xbuf, xs, half_at(odd), i, 1)
        jobs = []

        @pl.when(odd_now)
        def _(i=i):
            gram(xs, first, i, 1, own, second, 0, octs, XG, 1)

        jobs.append((odd_now, [(XG, i, octs - 1, octs + 1, 0, 1)]))

        @pl.when(even_now)
        def _(i=i):
            gram(scaled, first, 0, octs, xbuf, first, i, 1, OWN, 1)

        @pl.when(has_u)
        def _(i=i):
            to_lower(i).wait_recv()
            gram(scaled, first, i, octs - i, ubuf, first, i, 1, OWN, 2)

        @pl.when(jnp.logical_and(has_u, even_now))
        def _(i=i):
            gram(xs, first, i, 1, ubuf, first, 0, i + 1, XG, 1)
            if i:
                gram(xs, first, 0, i, ubuf, first, i, 1, XG, 1)

        jobs.append((jnp.logical_and(has_u, even_now), corner(XG, i)))

        @pl.when(has_d)
        def _(i=i):
            to_upper(i).wait_recv()
            scale(dbuf, ds, second, i, 1)
            gram(ds, first, i, 1, own, second, 0, i + 1, DG, 2)

        @pl.when(jnp.logical_and(has_d, odd_now))
        def _(i=i):
            gram(ds, first, i, 1, xbuf, first, 0, i + 1, DG, 1)
            if i:
                gram(ds, first, 0, i, xbuf, first, i, 1, DG, 1)

        jobs.append((jnp.logical_and(has_d, odd_now), corner(DG, i) + [(DG, i, 2 * octs, i, 0, 1)]))
        jobs.append((jnp.logical_and(has_d, even_now), [(DG, i, 2 * octs - 1, i + 1, 0, 1)]))
        own_even = [(OWN, 0, octs - 1 + i, octs, 1, 0)]
        if last:
            own_even.append((OWN, 0, 2 * octs - 1, octs, 1, 0))
        jobs.append((even_now, own_even))
        if i == 0:
            jobs.append((jnp.logical_and(has_u, odd_now), [(OWN, 0, 2 * octs - 1, octs, 1, 0)]))
        else:
            jobs.append((has_u, [(OWN, i, 2 * octs - 1 + i, octs - i, 1, 0)]))
        both_ways(jobs)

    def forward(slot, ff, o):
        return pltpu.make_async_remote_copy(
            src_ref=total.at[slot, rows_of(o), :], dst_ref=fwd.at[slot, rows_of(o), :],
            send_sem=gsend.at[slot, o], recv_sem=grecv.at[slot, o],
            device_id=dev(ff, p), device_id_type=MESH,
        )

    def settle(slot, target):
        def step(o, carry):
            here = valid(slot, o, p)

            @pl.when(here)
            def _():
                value = total[slot, rows_of(o), :]
                for hop in range(1, nz):
                    source = lax.rem(z + hop, nz)
                    z_copy(slot, o, z, source).wait_recv()
                    value = value + zin[slot, source, rows_of(o), :].astype(f32)
                total[slot, rows_of(o), :] = value
                if target is not None:
                    forward(slot, target, o).start()

            if target is None:
                @pl.when(jnp.logical_not(here))
                def _():
                    total[slot, rows_of(o), :] = jnp.zeros((oct_rows, LANES), f32)

            return carry

        lax.fori_loop(0, octs, step, 0)

    settle(XG, mate)
    settle(DG, f - 2)
    settle(OWN, None)

    def drain(slot):
        def step(i, carry):
            pp, o = i // octs, lax.rem(i, octs)
            zd = pp // CORES

            @pl.when(valid(slot, o, pp))
            def _():
                @pl.when(lax.rem(pp, CORES) != core)
                def _():
                    core_copy(slot, o, pp).wait_send()

                @pl.when(jnp.logical_and(lax.rem(pp, CORES) == core, z != zd))
                def _():
                    z_copy(slot, o, zd, z).wait_send()

            return carry

        lax.fori_loop(0, npan * octs, step, 0)

    for slot in (OWN, XG, DG):
        drain(slot)

    mate_gives = jnp.logical_or(odd == 0, f + 1 < nf)

    def take(slot, giver, comes):
        def step(o, carry):
            @pl.when(comes(o))
            def _():
                forward(slot, giver, o).wait_recv()
                total[OWN, rows_of(o), :] = total[OWN, rows_of(o), :] + fwd[slot, rows_of(o), :]

            return carry

        lax.fori_loop(0, octs, step, 0)

    def from_mate(o):
        t = o + p
        return jnp.logical_and(mate_gives, jnp.logical_and(t >= octs - 1, t <= 2 * octs - 1))

    def from_upper(o):
        t = o + p
        reach = jnp.logical_or(t >= 2 * octs - 1, jnp.logical_and(odd == 1, t >= octs - 1))
        return jnp.logical_and(has_u, reach)

    take(XG, mate, from_mate)
    take(DG, f - 2, from_upper)

    fin[...] = total[OWN]
    eye = lax.broadcasted_iota(jnp.int32, (freqs, freqs), 0) == lax.broadcasted_iota(
        jnp.int32, (freqs, freqs), 1
    )
    width = jnp.sum(
        jnp.where(eye, jnp.broadcast_to(bw_ref[...].astype(f32), (freqs, freqs)), 0.0), 1, keepdims=True
    )
    width = jnp.broadcast_to(width, (freqs, LANES))
    norm = jnp.float32(1.0 / math.sqrt(panels * npan))
    part = lax.broadcasted_iota(jnp.int32, (freqs, LANES), 1) // COMP
    for h in range(COMP // 8):
        values = [fin[pl.ds(h * 8 + a, freqs, stride=COMP), :] for a in range(8)]
        for bit in (1, 2, 4):
            upper = lax.rem(part // bit, 2) == 1
            fresh = list(values)
            for i in range(8):
                if i & bit:
                    continue
                j = i | bit
                fresh[i] = jnp.where(upper, pltpu.roll(values[j], COMP * bit, 1), values[i])
                fresh[j] = jnp.where(upper, values[j], pltpu.roll(values[i], LANES - COMP * bit, 1))
            values = fresh
        for k in range(8):
            offset = (p * 8 + k + 1).astype(f32)
            live = offset <= width
            start = (k * (COMP // 8) + h) * LANES
            out_ref[:, start:start + LANES] = jnp.where(live, values[k] * norm, 0.0)

    def close(o, carry):
        to_mate(o).wait_send()

        @pl.when(has_d)
        def _():
            to_lower(o).wait_send()

        @pl.when(has_u)
        def _():
            to_upper(o).wait_send()

        @pl.when(valid(XG, o, p))
        def _():
            forward(XG, mate, o).wait_send()

        @pl.when(valid(DG, o, p))
        def _():
            forward(DG, f - 2, o).wait_send()

        return carry

    lax.fori_loop(0, octs, close, 0)


def fused(nf, npan, fields, quad_index, band_width):
    freqs, comp, panels = fields.shape
    rows = freqs * comp
    nz = npan // CORES
    half = panels // 2
    octs = freqs // 8
    out_cols = REACH * freqs * comp * comp // npan
    bf16, f32 = jnp.bfloat16, jnp.float32
    dma = pltpu.SemaphoreType.DMA
    vmem = pl.BlockSpec(memory_space=pltpu.VMEM)
    return pl.pallas_call(
        functools.partial(kernel, nf, npan),
        out_shape=jax.ShapeDtypeStruct((freqs, out_cols), f32),
        in_specs=[pl.BlockSpec(memory_space=pl.ANY), vmem, vmem],
        out_specs=vmem,
        scratch_shapes=[
            pltpu.VMEM((rows, panels), bf16),
            pltpu.VMEM((rows, panels), bf16),
            pltpu.VMEM((rows, half), bf16),
            pltpu.VMEM((rows, half), bf16),
            pltpu.VMEM((rows, half), bf16),
            pltpu.VMEM((rows, half), bf16),
            pltpu.VMEM((rows, half), bf16),
            pltpu.VMEM((3, rows, (REACH + 1) * rows), f32),
            pltpu.VMEM((3, npan, rows, LANES), f32),
            pltpu.VMEM((3, npan, rows, LANES), bf16),
            pltpu.VMEM((3, nz, rows, LANES), bf16),
            pltpu.VMEM((3, nz, rows, LANES), bf16),
            pltpu.VMEM((3, nz, rows, LANES), bf16),
            pltpu.VMEM((3, rows, LANES), f32),
            pltpu.VMEM((3, rows, LANES), f32),
            pltpu.VMEM((rows, LANES), f32),
            dma,
            dma((3, octs)), dma((3, octs)),
            dma((3, nz, octs)), dma((3, nz, octs)),
            dma((3, nz, octs)), dma((3, nz, octs)),
            dma((3, octs)), dma((3, octs)),
        ],
        compiler_params=pltpu.CompilerParams(
            collective_id=0, has_side_effects=True, vmem_limit_bytes=58 * 1024 * 1024
        ),
    )(fields.reshape(rows, panels), quad_index.reshape(1, panels), band_width.reshape(1, freqs))


def local(nf, npan, fields, quad_index, band_width):
    freqs, comp, panels = fields.shape
    share = REACH * freqs * comp // npan
    fits = nf % 2 == 0 and npan % CORES == 0 and share == LANES and freqs % 8 == 0 and panels % (4 * LANES) == 0
    if not fits:
        return plain(fields, quad_index, band_width)
    return fused(nf, npan, fields, quad_index, band_width)


def solution(mesh):
    placed = (P("freq", None, "panel"), P("panel"), P("freq"))
    return jax.shard_map(
        functools.partial(local, mesh.shape["freq"], mesh.shape["panel"]),
        mesh=mesh, in_specs=placed, out_specs=P("freq", "panel"), check_vma=False,
    )
```

```python
import functools
import math

import jax
import jax.numpy as jnp
from jax import lax
from jax.experimental import pallas as pl
from jax.experimental.pallas import tpu as pltpu
from jax.sharding import PartitionSpec as P

COMP = 16
REACH = 2
LANES = 128
CORES = 2
MESH = pl.DeviceIdType.MESH

QUAD_TABLE = (0.2, 0.45, 0.8, 1.1, 1.6, 2.3)


def shifted(x, axis, by):
    devices = lax.axis_size(axis)
    pairs = [(i, i + by) for i in range(devices) if 0 <= i + by < devices]
    return lax.ppermute(x, axis, pairs)


def plain(fields, quad_index, band_width):
    freq_local = fields.shape[0]
    panel_local = fields.shape[2]
    band = REACH * freq_local
    table = jnp.asarray(QUAD_TABLE, jnp.float32)
    matches = quad_index[None, :] == jnp.arange(6, dtype=jnp.int32)[:, None]
    weight = jnp.sum(jnp.where(matches, table[:, None], jnp.float32(0.0)), 0)
    scaled = (fields.astype(jnp.float32) * weight).astype(jnp.bfloat16)
    own_rows = scaled.reshape(freq_local * COMP, panel_local)
    partners = [fields]
    for distance in range(1, REACH + 1):
        partners.append(shifted(fields, "freq", -distance))
    grams = []
    for partner in partners:
        grams.append(
            lax.dot_general(
                own_rows,
                partner.reshape(freq_local * COMP, panel_local),
                (((1,), (1,)), ((), ())),
                preferred_element_type=jnp.float32,
            )
        )
    stacked = jnp.concatenate(grams, 1).reshape(freq_local, COMP, (REACH + 1) * freq_local, COMP)

    def pick_band(block, row_index):
        return lax.dynamic_slice_in_dim(block, row_index + 1, band, 1)

    picked = jax.vmap(pick_band)(stacked, jnp.arange(freq_local, dtype=jnp.int32))
    picked = picked.transpose(0, 2, 1, 3)
    offsets = jnp.arange(band, dtype=jnp.int32) + 1
    live_mask = offsets[None, :] <= band_width[:, None]
    picked = jnp.where(live_mask[:, :, None, None], picked, jnp.float32(0.0))
    panels_total = panel_local * lax.axis_size("panel")
    terms = picked.reshape(freq_local, band * COMP * COMP) * jnp.float32(
        1.0 / math.sqrt(panels_total)
    )
    return lax.psum_scatter(terms, "panel", scatter_dimension=1, tiled=True)


OWN, XG, DG = 0, 1, 2


def kernel(
    nf, npan, f_hbm, q_ref, bw_ref, out_ref,
    own, scaled, xbuf, ubuf, dbuf, xs, ds, acc, keep, away, cxin, zout, zin, total, fwd, fin,
    local_sem, fsend, frecv, csend, crecv, zsend, zrecv, gsend, grecv,
):
    rows, panels = own.shape
    half = panels // 2
    block = rows
    freqs = rows // COMP
    oct_rows = 8 * COMP
    octs = rows // oct_rows
    nz = npan // CORES
    f32, bf16 = jnp.float32, jnp.bfloat16

    f = lax.axis_index("freq")
    p = lax.axis_index("panel")
    z, core = p // CORES, lax.rem(p, CORES)
    odd = lax.rem(f, 2)
    mate = f + 1 - 2 * odd
    has_u = f + 2 < nf
    has_d = f >= 2
    has_x = jnp.logical_or(odd == 1, has_u)
    partner = p + 1 - 2 * core

    def dev(ff, pp):
        return {"freq": ff, "panel": pp}

    load = pltpu.make_async_copy(f_hbm, own, local_sem)
    load.start()

    barrier = pltpu.get_barrier_semaphore()

    def greet(ff, pp):
        pl.semaphore_signal(barrier, inc=1, device_id=dev(ff, pp), device_id_type=MESH)

    greet(mate, p)
    greet(f, partner)
    for zd in range(nz):
        @pl.when(z != zd)
        def _(zd=zd):
            greet(f, zd * CORES + core)

    @pl.when(has_u)
    def _():
        greet(f + 2, p)

    @pl.when(has_d)
    def _():
        greet(f - 2, p)

    count = 1 + nz + jnp.where(has_u, 1, 0) + jnp.where(has_d, 1, 0)
    pl.semaphore_wait(barrier, count)

    def half_at(which):
        return pl.ds(pl.multiple_of(which * half, LANES), half)

    def rows_of(o, n=1):
        return pl.ds(pl.multiple_of(o * oct_rows, oct_rows), n * oct_rows)

    def field_copy(which, dst, slot, ff, o):
        return pltpu.make_async_remote_copy(
            src_ref=f_hbm.at[rows_of(o), half_at(which)], dst_ref=dst.at[rows_of(o), :],
            send_sem=fsend.at[slot, o], recv_sem=frecv.at[slot, o],
            device_id=dev(ff, p), device_id_type=MESH,
        )

    def to_mate(o):
        return field_copy(1 - odd, xbuf, 0, mate, o)

    def to_lower(o):
        return field_copy(0, ubuf, 1, f - 2, o)

    def to_upper(o):
        return field_copy(1, dbuf, 2, f + 2, o)

    for o in range(octs):
        to_mate(octs - 1 - o).start()

        @pl.when(has_d)
        def _(o=o):
            to_lower(o).start()

        @pl.when(has_u)
        def _(o=o):
            to_upper(octs - 1 - o).start()

    def weight_at(where):
        index = q_ref[:, where]
        w = jnp.zeros(index.shape, f32)
        for value, entry in enumerate(QUAD_TABLE):
            w = jnp.where(index == value, jnp.float32(entry), w)
        return w

    def scale(src, dst, where, o, n):
        w = weight_at(where)

        def step(i, carry):
            at = pl.ds(pl.multiple_of(o * oct_rows + i * 32, 32), 32)
            dst[at, :] = (src[at, :].astype(f32) * w).astype(bf16)
            return carry

        lax.fori_loop(0, n * oct_rows // 32, step, 0)

    def gram(left, left_at, lo, n, right, right_at, ro, m, slot, rel):
        tall = 2 if n % 2 == 0 else 1
        first_col = rel * block + ro * oct_rows

        def step(i, carry):
            at = rows_of(lo + i * tall, tall)
            acc[slot, at, first_col:first_col + m * oct_rows] = lax.dot_general(
                left[at, left_at], right[ro * oct_rows:(ro + m) * oct_rows, right_at],
                (((1,), (1,)), ((), ())), preferred_element_type=f32,
            )
            return carry

        if n == tall:
            step(0, 0)
        else:
            lax.fori_loop(0, n // tall, step, 0)

    def clear(slot, tile):
        acc[slot, :, tile * LANES:(tile + 1) * LANES] = jnp.zeros((rows, LANES), f32)

    clear(XG, octs - 1)
    clear(XG, 2 * octs)
    clear(DG, octs - 1)

    @pl.when(odd == 0)
    def _():
        clear(DG, 2 * octs - 1)

    @pl.when(odd == 1)
    def _():
        clear(OWN, octs)
        clear(OWN, 2 * octs - 1)

    @pl.when(jnp.logical_not(has_u))
    def _():
        clear(OWN, 2 * octs)

    def valid(slot, o, pp):
        t = o + pp
        low, high = t >= octs - 1, t <= 2 * octs - 1
        if slot == OWN:
            return jnp.logical_or(
                t <= octs - 1,
                jnp.logical_or(
                    jnp.logical_and(odd == 0, high),
                    jnp.logical_and(has_u, t >= 2 * octs - 1),
                ),
            )
        if slot == XG:
            return jnp.logical_and(has_x, jnp.logical_and(low, high))
        upper = jnp.logical_or(t >= 2 * octs - 1, jnp.logical_and(odd == 1, low))
        return jnp.logical_and(has_d, upper)

    def core_copy(slot, o, pp):
        zd = pp // CORES
        return pltpu.make_async_remote_copy(
            src_ref=away.at[slot, pp, rows_of(o), :], dst_ref=cxin.at[slot, zd, rows_of(o), :],
            send_sem=csend.at[slot, zd, o], recv_sem=crecv.at[slot, zd, o],
            device_id=dev(f, partner), device_id_type=MESH,
        )

    def z_copy(slot, o, zd, source):
        return pltpu.make_async_remote_copy(
            src_ref=zout.at[slot, zd, rows_of(o), :], dst_ref=zin.at[slot, source, rows_of(o), :],
            send_sem=zsend.at[slot, zd, o], recv_sem=zrecv.at[slot, source, o],
            device_id=dev(f, zd * CORES + core), device_id_type=MESH,
        )

    def walk(act, slot, o, t, n, do, dt):
        def step(i, carry):
            oo, tt = o + i * do, t + i * dt
            act(slot, oo, tt - oo, tt)
            return carry

        if n > 0:
            lax.fori_loop(0, n, step, 0)

    def make(slot, o, pp, t):
        lane = pl.multiple_of(t * LANES, LANES)
        for c in range(8):
            at = pl.ds(pl.multiple_of(o * oct_rows + c * COMP, COMP), COMP)
            if c == 7:
                value = acc[slot, at, pl.ds(pl.multiple_of(lane + LANES, LANES), LANES)]
            else:
                pair = acc[slot, at, pl.ds(lane, 2 * LANES)]
                value = pltpu.roll(pair, 2 * LANES - COMP * (c + 1), 1)[:, :LANES]
            keep[slot, pp, at, :] = value
            away[slot, pp, at, :] = value.astype(bf16)

        @pl.when(lax.rem(pp, CORES) != core)
        def _():
            core_copy(slot, o, pp).start()

    def join(slot, o, pp, t):
        @pl.when(lax.rem(pp, CORES) == core)
        def _():
            zd = pp // CORES
            core_copy(slot, o, pp).wait_recv()
            both = keep[slot, pp, rows_of(o), :] + cxin[slot, zd, rows_of(o), :].astype(f32)

            @pl.when(z == zd)
            def _():
                total[slot, rows_of(o), :] = both

            @pl.when(z != zd)
            def _():
                zout[slot, zd, rows_of(o), :] = both.astype(bf16)
                z_copy(slot, o, zd, z).start()

    def both_ways(jobs):
        for act in (make, join):
            for job in jobs:
                if len(job) == 2:
                    @pl.when(job[0])
                    def _(job=job, act=act):
                        for inner in job[1]:
                            walk(act, *inner)
                else:
                    walk(act, *job)

    load.wait()
    everything = pl.ds(0, panels)
    first = pl.ds(0, half)
    second = pl.ds(half, half)
    even_now, odd_now = odd == 0, odd == 1
    scale(own, scaled, everything, 0, octs)
    gram(scaled, everything, 0, octs, own, everything, 0, octs, OWN, 0)
    jobs = [(OWN, 0, t, t + 1, 1, 0) for t in range(octs - 1)]
    jobs.append((odd_now, [(OWN, 0, octs - 1, octs, 1, 0)]))
    both_ways(jobs)

    for i in range(octs):
        x = octs - 1 - i
        last = i == octs - 1
        to_mate(x).wait_recv()
        scale(xbuf, xs, half_at(odd), x, 1)
        jobs = []

        @pl.when(odd_now)
        def _(x=x):
            gram(xs, first, x, 1, own, second, 0, octs, XG, 1)

        jobs.append((odd_now, [(XG, x, octs - 1, octs + 1, 0, 1)]))

        @pl.when(even_now)
        def _(x=x):
            gram(scaled, first, 0, octs, xbuf, first, x, 1, OWN, 1)

        @pl.when(has_u)
        def _(i=i):
            to_lower(i).wait_recv()
            gram(scaled, first, i, octs - i, ubuf, first, i, 1, OWN, 2)

        @pl.when(jnp.logical_and(has_u, even_now))
        def _(i=i, x=x):
            gram(xs, first, x, 1, ubuf, first, 0, i + 1, XG, 1)
            if i:
                gram(xs, first, x + 1, i, ubuf, first, i, 1, XG, 1)

        mixed = [(XG, x, octs - 1, i + 1 + last, 0, 1), (XG, x + 1, octs - 1 + i, i, 1, 0)]
        if last:
            mixed.append((XG, x + 1, 2 * octs - 1, i, 1, 0))
        jobs.append((jnp.logical_and(has_u, even_now), mixed))

        @pl.when(has_d)
        def _(x=x):
            to_upper(x).wait_recv()
            scale(dbuf, ds, second, x, 1)
            gram(ds, first, x, 1, own, second, 0, x + 1, DG, 2)

        @pl.when(jnp.logical_and(has_d, odd_now))
        def _(i=i, x=x):
            gram(ds, first, x, 1, xbuf, first, x, i + 1, DG, 1)
            if i:
                gram(ds, first, x + 1, i, xbuf, first, x, 1, DG, 1)

        mixed = [
            (DG, x, octs + x - last, i + 1 + last, 0, 1),
            (DG, x + 1, octs + x, i, 1, 0),
            (DG, x, 2 * octs, x, 0, 1),
        ]
        if last:
            mixed.append((DG, x + 1, octs - 1, i, 1, 0))
        jobs.append((jnp.logical_and(has_d, odd_now), mixed))
        jobs.append((jnp.logical_and(has_d, even_now), [(DG, x, 2 * octs - 1, x + 1, 0, 1)]))
        own_even = [(OWN, 0, octs + x, octs, 1, 0)]
        if last:
            own_even.append((OWN, 0, octs - 1, octs, 1, 0))
        jobs.append((even_now, own_even))
        if i == 0:
            jobs.append((jnp.logical_and(has_u, odd_now), [(OWN, 0, 2 * octs - 1, octs, 1, 0)]))
        else:
            jobs.append((has_u, [(OWN, i, 2 * octs - 1 + i, octs - i, 1, 0)]))
        both_ways(jobs)

    def forward(slot, ff, o):
        return pltpu.make_async_remote_copy(
            src_ref=total.at[slot, rows_of(o), :], dst_ref=fwd.at[slot, rows_of(o), :],
            send_sem=gsend.at[slot, o], recv_sem=grecv.at[slot, o],
            device_id=dev(ff, p), device_id_type=MESH,
        )

    def settle(slot, target):
        def step(o, carry):
            here = valid(slot, o, p)

            @pl.when(here)
            def _():
                value = total[slot, rows_of(o), :]
                for hop in range(1, nz):
                    source = lax.rem(z + hop, nz)
                    z_copy(slot, o, z, source).wait_recv()
                    value = value + zin[slot, source, rows_of(o), :].astype(f32)
                total[slot, rows_of(o), :] = value
                if target is not None:
                    forward(slot, target, o).start()

            if target is None:
                @pl.when(jnp.logical_not(here))
                def _():
                    total[slot, rows_of(o), :] = jnp.zeros((oct_rows, LANES), f32)

            return carry

        lax.fori_loop(0, octs, step, 0)

    settle(XG, mate)
    settle(DG, f - 2)
    settle(OWN, None)

    def drain(slot):
        def step(i, carry):
            pp, o = i // octs, lax.rem(i, octs)
            zd = pp // CORES

            @pl.when(valid(slot, o, pp))
            def _():
                @pl.when(lax.rem(pp, CORES) != core)
                def _():
                    core_copy(slot, o, pp).wait_send()

                @pl.when(jnp.logical_and(lax.rem(pp, CORES) == core, z != zd))
                def _():
                    z_copy(slot, o, zd, z).wait_send()

            return carry

        lax.fori_loop(0, npan * octs, step, 0)

    for slot in (OWN, XG, DG):
        drain(slot)

    mate_gives = jnp.logical_or(odd == 0, f + 1 < nf)

    def take(slot, giver, comes):
        def step(o, carry):
            @pl.when(comes(o))
            def _():
                forward(slot, giver, o).wait_recv()
                total[OWN, rows_of(o), :] = total[OWN, rows_of(o), :] + fwd[slot, rows_of(o), :]

            return carry

        lax.fori_loop(0, octs, step, 0)

    def from_mate(o):
        t = o + p
        return jnp.logical_and(mate_gives, jnp.logical_and(t >= octs - 1, t <= 2 * octs - 1))

    def from_upper(o):
        t = o + p
        reach = jnp.logical_or(t >= 2 * octs - 1, jnp.logical_and(odd == 1, t >= octs - 1))
        return jnp.logical_and(has_u, reach)

    take(XG, mate, from_mate)
    take(DG, f - 2, from_upper)

    fin[...] = total[OWN]
    eye = lax.broadcasted_iota(jnp.int32, (freqs, freqs), 0) == lax.broadcasted_iota(
        jnp.int32, (freqs, freqs), 1
    )
    width = jnp.sum(
        jnp.where(eye, jnp.broadcast_to(bw_ref[...].astype(f32), (freqs, freqs)), 0.0), 1, keepdims=True
    )
    width = jnp.broadcast_to(width, (freqs, LANES))
    norm = jnp.float32(1.0 / math.sqrt(panels * npan))
    part = lax.broadcasted_iota(jnp.int32, (freqs, LANES), 1) // COMP
    for h in range(COMP // 8):
        values = [fin[pl.ds(h * 8 + a, freqs, stride=COMP), :] for a in range(8)]
        for bit in (1, 2, 4):
            upper = lax.rem(part // bit, 2) == 1
            fresh = list(values)
            for i in range(8):
                if i & bit:
                    continue
                j = i | bit
                fresh[i] = jnp.where(upper, pltpu.roll(values[j], COMP * bit, 1), values[i])
                fresh[j] = jnp.where(upper, values[j], pltpu.roll(values[i], LANES - COMP * bit, 1))
            values = fresh
        for k in range(8):
            offset = (p * 8 + k + 1).astype(f32)
            live = offset <= width
            start = (k * (COMP // 8) + h) * LANES
            out_ref[:, start:start + LANES] = jnp.where(live, values[k] * norm, 0.0)

    def close(o, carry):
        to_mate(o).wait_send()

        @pl.when(has_d)
        def _():
            to_lower(o).wait_send()

        @pl.when(has_u)
        def _():
            to_upper(o).wait_send()

        @pl.when(valid(XG, o, p))
        def _():
            forward(XG, mate, o).wait_send()

        @pl.when(valid(DG, o, p))
        def _():
            forward(DG, f - 2, o).wait_send()

        return carry

    lax.fori_loop(0, octs, close, 0)


def fused(nf, npan, fields, quad_index, band_width):
    freqs, comp, panels = fields.shape
    rows = freqs * comp
    nz = npan // CORES
    half = panels // 2
    octs = freqs // 8
    out_cols = REACH * freqs * comp * comp // npan
    bf16, f32 = jnp.bfloat16, jnp.float32
    dma = pltpu.SemaphoreType.DMA
    vmem = pl.BlockSpec(memory_space=pltpu.VMEM)
    return pl.pallas_call(
        functools.partial(kernel, nf, npan),
        out_shape=jax.ShapeDtypeStruct((freqs, out_cols), f32),
        in_specs=[pl.BlockSpec(memory_space=pl.ANY), vmem, vmem],
        out_specs=vmem,
        scratch_shapes=[
            pltpu.VMEM((rows, panels), bf16),
            pltpu.VMEM((rows, panels), bf16),
            pltpu.VMEM((rows, half), bf16),
            pltpu.VMEM((rows, half), bf16),
            pltpu.VMEM((rows, half), bf16),
            pltpu.VMEM((rows, half), bf16),
            pltpu.VMEM((rows, half), bf16),
            pltpu.VMEM((3, rows, (REACH + 1) * rows), f32),
            pltpu.VMEM((3, npan, rows, LANES), f32),
            pltpu.VMEM((3, npan, rows, LANES), bf16),
            pltpu.VMEM((3, nz, rows, LANES), bf16),
            pltpu.VMEM((3, nz, rows, LANES), bf16),
            pltpu.VMEM((3, nz, rows, LANES), bf16),
            pltpu.VMEM((3, rows, LANES), f32),
            pltpu.VMEM((3, rows, LANES), f32),
            pltpu.VMEM((rows, LANES), f32),
            dma,
            dma((3, octs)), dma((3, octs)),
            dma((3, nz, octs)), dma((3, nz, octs)),
            dma((3, nz, octs)), dma((3, nz, octs)),
            dma((3, octs)), dma((3, octs)),
        ],
        compiler_params=pltpu.CompilerParams(
            collective_id=0, has_side_effects=True, vmem_limit_bytes=58 * 1024 * 1024
        ),
    )(fields.reshape(rows, panels), quad_index.reshape(1, panels), band_width.reshape(1, freqs))


def local(nf, npan, fields, quad_index, band_width):
    freqs, comp, panels = fields.shape
    share = REACH * freqs * comp // npan
    fits = nf % 2 == 0 and npan % CORES == 0 and share == LANES and freqs % 8 == 0 and panels % (4 * LANES) == 0
    if not fits:
        return plain(fields, quad_index, band_width)
    return fused(nf, npan, fields, quad_index, band_width)


def solution(mesh):
    placed = (P("freq", None, "panel"), P("panel"), P("freq"))
    return jax.shard_map(
        functools.partial(local, mesh.shape["freq"], mesh.shape["panel"]),
        mesh=mesh, in_specs=placed, out_specs=P("freq", "panel"), check_vma=False,
    )
```

```python
import functools
import math

import jax
import jax.numpy as jnp
from jax import lax
from jax.experimental import pallas as pl
from jax.experimental.pallas import tpu as pltpu
from jax.sharding import PartitionSpec as P

COMP = 16
REACH = 2
LANES = 128
CORES = 2
MESH = pl.DeviceIdType.MESH

QUAD_TABLE = (0.2, 0.45, 0.8, 1.1, 1.6, 2.3)


def shifted(x, axis, by):
    devices = lax.axis_size(axis)
    pairs = [(i, i + by) for i in range(devices) if 0 <= i + by < devices]
    return lax.ppermute(x, axis, pairs)


def plain(fields, quad_index, band_width):
    freq_local = fields.shape[0]
    panel_local = fields.shape[2]
    band = REACH * freq_local
    table = jnp.asarray(QUAD_TABLE, jnp.float32)
    matches = quad_index[None, :] == jnp.arange(6, dtype=jnp.int32)[:, None]
    weight = jnp.sum(jnp.where(matches, table[:, None], jnp.float32(0.0)), 0)
    scaled = (fields.astype(jnp.float32) * weight).astype(jnp.bfloat16)
    own_rows = scaled.reshape(freq_local * COMP, panel_local)
    partners = [fields]
    for distance in range(1, REACH + 1):
        partners.append(shifted(fields, "freq", -distance))
    grams = []
    for partner in partners:
        grams.append(
            lax.dot_general(
                own_rows,
                partner.reshape(freq_local * COMP, panel_local),
                (((1,), (1,)), ((), ())),
                preferred_element_type=jnp.float32,
            )
        )
    stacked = jnp.concatenate(grams, 1).reshape(freq_local, COMP, (REACH + 1) * freq_local, COMP)

    def pick_band(block, row_index):
        return lax.dynamic_slice_in_dim(block, row_index + 1, band, 1)

    picked = jax.vmap(pick_band)(stacked, jnp.arange(freq_local, dtype=jnp.int32))
    picked = picked.transpose(0, 2, 1, 3)
    offsets = jnp.arange(band, dtype=jnp.int32) + 1
    live_mask = offsets[None, :] <= band_width[:, None]
    picked = jnp.where(live_mask[:, :, None, None], picked, jnp.float32(0.0))
    panels_total = panel_local * lax.axis_size("panel")
    terms = picked.reshape(freq_local, band * COMP * COMP) * jnp.float32(
        1.0 / math.sqrt(panels_total)
    )
    return lax.psum_scatter(terms, "panel", scatter_dimension=1, tiled=True)


OWN, XG, DG = 0, 1, 2


def kernel(
    nf, npan, f_hbm, q_ref, bw_ref, out_ref,
    own, scaled, xbuf, ubuf, dbuf, xs, ds, acc, keep, away, cxin, zout, zin, total, fwd, fin,
    local_sem, fsend, frecv, csend, crecv, zsend, zrecv, gsend, grecv,
):
    rows, panels = own.shape
    half = panels // 2
    block = rows
    freqs = rows // COMP
    oct_rows = 8 * COMP
    octs = rows // oct_rows
    nz = npan // CORES
    f32, bf16 = jnp.float32, jnp.bfloat16

    f = lax.axis_index("freq")
    p = lax.axis_index("panel")
    z, core = p // CORES, lax.rem(p, CORES)
    odd = lax.rem(f, 2)
    mate = f + 1 - 2 * odd
    has_u = f + 2 < nf
    has_d = f >= 2
    has_x = jnp.logical_or(odd == 1, has_u)
    partner = p + 1 - 2 * core

    def dev(ff, pp):
        return {"freq": ff, "panel": pp}

    load = pltpu.make_async_copy(f_hbm, own, local_sem)
    load.start()

    barrier = pltpu.get_barrier_semaphore()

    def greet(ff, pp):
        pl.semaphore_signal(barrier, inc=1, device_id=dev(ff, pp), device_id_type=MESH)

    greet(mate, p)
    greet(f, partner)
    for zd in range(nz):
        @pl.when(z != zd)
        def _(zd=zd):
            greet(f, zd * CORES + core)

    @pl.when(has_u)
    def _():
        greet(f + 2, p)

    @pl.when(has_d)
    def _():
        greet(f - 2, p)

    count = 1 + nz + jnp.where(has_u, 1, 0) + jnp.where(has_d, 1, 0)
    pl.semaphore_wait(barrier, count)

    def half_at(which):
        return pl.ds(pl.multiple_of(which * half, LANES), half)

    def rows_of(o, n=1):
        return pl.ds(pl.multiple_of(o * oct_rows, oct_rows), n * oct_rows)

    def field_copy(which, dst, slot, ff, o):
        return pltpu.make_async_remote_copy(
            src_ref=f_hbm.at[rows_of(o), half_at(which)], dst_ref=dst.at[rows_of(o), :],
            send_sem=fsend.at[slot, o], recv_sem=frecv.at[slot, o],
            device_id=dev(ff, p), device_id_type=MESH,
        )

    def to_mate(o):
        return field_copy(1 - odd, xbuf, 0, mate, o)

    def to_lower(o):
        return field_copy(0, ubuf, 1, f - 2, o)

    def to_upper(o):
        return field_copy(1, dbuf, 2, f + 2, o)

    for o in range(octs):
        to_mate(octs - 1 - o).start()

        @pl.when(has_d)
        def _(o=o):
            to_lower(o).start()

        @pl.when(has_u)
        def _(o=o):
            to_upper(octs - 1 - o).start()

    def weight_at(where):
        index = q_ref[:, where]
        w = jnp.zeros(index.shape, f32)
        for value, entry in enumerate(QUAD_TABLE):
            w = jnp.where(index == value, jnp.float32(entry), w)
        return w

    def scale(src, dst, where, o, n):
        w = weight_at(where)

        def step(i, carry):
            at = pl.ds(pl.multiple_of(o * oct_rows + i * 32, 32), 32)
            dst[at, :] = (src[at, :].astype(f32) * w).astype(bf16)
            return carry

        lax.fori_loop(0, n * oct_rows // 32, step, 0)

    def gram(left, left_at, lo, n, right, right_at, ro, m, slot, rel):
        tall = 2 if n % 2 == 0 else 1
        first_col = rel * block + ro * oct_rows

        def step(i, carry):
            at = rows_of(lo + i * tall, tall)
            acc[slot, at, first_col:first_col + m * oct_rows] = lax.dot_general(
                left[at, left_at], right[ro * oct_rows:(ro + m) * oct_rows, right_at],
                (((1,), (1,)), ((), ())), preferred_element_type=f32,
            )
            return carry

        if n == tall:
            step(0, 0)
        else:
            lax.fori_loop(0, n // tall, step, 0)

    def clear(slot, tile):
        acc[slot, :, tile * LANES:(tile + 1) * LANES] = jnp.zeros((rows, LANES), f32)

    clear(XG, octs - 1)
    clear(XG, 2 * octs)
    clear(DG, octs - 1)

    @pl.when(odd == 0)
    def _():
        clear(DG, 2 * octs - 1)

    @pl.when(odd == 1)
    def _():
        clear(OWN, octs)
        clear(OWN, 2 * octs - 1)

    @pl.when(jnp.logical_not(has_u))
    def _():
        clear(OWN, 2 * octs)

    def valid(slot, o, pp):
        t = o + pp
        low, high = t >= octs - 1, t <= 2 * octs - 1
        if slot == OWN:
            return jnp.logical_or(
                t <= octs - 1,
                jnp.logical_or(
                    jnp.logical_and(odd == 0, high),
                    jnp.logical_and(has_u, t >= 2 * octs - 1),
                ),
            )
        if slot == XG:
            return jnp.logical_and(has_x, jnp.logical_and(low, high))
        upper = jnp.logical_or(t >= 2 * octs - 1, jnp.logical_and(odd == 1, low))
        return jnp.logical_and(has_d, upper)

    def core_copy(slot, o, pp):
        zd = pp // CORES
        return pltpu.make_async_remote_copy(
            src_ref=away.at[slot, pp, rows_of(o), :], dst_ref=cxin.at[slot, zd, rows_of(o), :],
            send_sem=csend.at[slot, zd, o], recv_sem=crecv.at[slot, zd, o],
            device_id=dev(f, partner), device_id_type=MESH,
        )

    def z_copy(slot, o, zd, source):
        return pltpu.make_async_remote_copy(
            src_ref=zout.at[slot, zd, rows_of(o), :], dst_ref=zin.at[slot, source, rows_of(o), :],
            send_sem=zsend.at[slot, zd, o], recv_sem=zrecv.at[slot, source, o],
            device_id=dev(f, zd * CORES + core), device_id_type=MESH,
        )

    def walk(act, slot, o, t, n, do, dt):
        def step(i, carry):
            oo, tt = o + i * do, t + i * dt
            act(slot, oo, tt - oo, tt)
            return carry

        if n > 0:
            lax.fori_loop(0, n, step, 0)

    def make(slot, o, pp, t):
        lane = pl.multiple_of(t * LANES, LANES)
        for c in range(8):
            at = pl.ds(pl.multiple_of(o * oct_rows + c * COMP, COMP), COMP)
            if c == 7:
                value = acc[slot, at, pl.ds(pl.multiple_of(lane + LANES, LANES), LANES)]
            else:
                pair = acc[slot, at, pl.ds(lane, 2 * LANES)]
                value = pltpu.roll(pair, 2 * LANES - COMP * (c + 1), 1)[:, :LANES]
            keep[slot, pp, at, :] = value
            away[slot, pp, at, :] = value.astype(bf16)

        @pl.when(lax.rem(pp, CORES) != core)
        def _():
            core_copy(slot, o, pp).start()

    def join(slot, o, pp, t):
        @pl.when(lax.rem(pp, CORES) == core)
        def _():
            zd = pp // CORES
            core_copy(slot, o, pp).wait_recv()
            both = keep[slot, pp, rows_of(o), :] + cxin[slot, zd, rows_of(o), :].astype(f32)

            @pl.when(z == zd)
            def _():
                total[slot, rows_of(o), :] = both

            @pl.when(z != zd)
            def _():
                zout[slot, zd, rows_of(o), :] = both.astype(bf16)
                z_copy(slot, o, zd, z).start()

    def both_ways(jobs):
        flat = []
        for job in jobs:
            if len(job) == 2:
                flat.extend((job[0], inner) for inner in job[1] if inner[3] > 0)
            else:
                flat.append((None, job))

        def run(act, entry):
            when, inner = entry
            if when is None:
                walk(act, *inner)
            else:
                pl.when(when)(functools.partial(walk, act, *inner))

        previous = {}
        for entry in flat:
            role = id(entry[0])
            run(make, entry)
            if role in previous:
                run(join, previous[role])
            previous[role] = entry
        for entry in flat:
            if previous[id(entry[0])] is entry:
                run(join, entry)

    load.wait()
    everything = pl.ds(0, panels)
    first = pl.ds(0, half)
    second = pl.ds(half, half)
    even_now, odd_now = odd == 0, odd == 1
    scale(own, scaled, everything, 0, octs)
    gram(scaled, everything, 0, octs, own, everything, 0, octs, OWN, 0)
    jobs = [(OWN, 0, t, t + 1, 1, 0) for t in range(octs - 1)]
    jobs.append((odd_now, [(OWN, 0, octs - 1, octs, 1, 0)]))
    both_ways(jobs)

    for i in range(octs):
        x = octs - 1 - i
        last = i == octs - 1
        to_mate(x).wait_recv()
        scale(xbuf, xs, half_at(odd), x, 1)
        jobs = []

        @pl.when(odd_now)
        def _(x=x):
            gram(xs, first, x, 1, own, second, 0, octs, XG, 1)

        jobs.append((odd_now, [(XG, x, octs - 1, octs + 1, 0, 1)]))

        @pl.when(even_now)
        def _(x=x):
            gram(scaled, first, 0, octs, xbuf, first, x, 1, OWN, 1)

        @pl.when(has_u)
        def _(i=i):
            to_lower(i).wait_recv()
            gram(scaled, first, i, octs - i, ubuf, first, i, 1, OWN, 2)

        @pl.when(jnp.logical_and(has_u, even_now))
        def _(i=i, x=x):
            gram(xs, first, x, 1, ubuf, first, 0, i + 1, XG, 1)
            if i:
                gram(xs, first, x + 1, i, ubuf, first, i, 1, XG, 1)

        mixed = [(XG, x, octs - 1, i + 1 + last, 0, 1), (XG, x + 1, octs - 1 + i, i, 1, 0)]
        if last:
            mixed.append((XG, x + 1, 2 * octs - 1, i, 1, 0))
        jobs.append((jnp.logical_and(has_u, even_now), mixed))

        @pl.when(has_d)
        def _(x=x):
            to_upper(x).wait_recv()
            scale(dbuf, ds, second, x, 1)
            gram(ds, first, x, 1, own, second, 0, x + 1, DG, 2)

        @pl.when(jnp.logical_and(has_d, odd_now))
        def _(i=i, x=x):
            gram(ds, first, x, 1, xbuf, first, x, i + 1, DG, 1)
            if i:
                gram(ds, first, x + 1, i, xbuf, first, x, 1, DG, 1)

        mixed = [
            (DG, x, octs + x - last, i + 1 + last, 0, 1),
            (DG, x + 1, octs + x, i, 1, 0),
            (DG, x, 2 * octs, x, 0, 1),
        ]
        if last:
            mixed.append((DG, x + 1, octs - 1, i, 1, 0))
        jobs.append((jnp.logical_and(has_d, odd_now), mixed))
        jobs.append((jnp.logical_and(has_d, even_now), [(DG, x, 2 * octs - 1, x + 1, 0, 1)]))
        own_even = [(OWN, 0, octs + x, octs, 1, 0)]
        if last:
            own_even.append((OWN, 0, octs - 1, octs, 1, 0))
        jobs.append((even_now, own_even))
        if i == 0:
            jobs.append((jnp.logical_and(has_u, odd_now), [(OWN, 0, 2 * octs - 1, octs, 1, 0)]))
        else:
            jobs.append((has_u, [(OWN, i, 2 * octs - 1 + i, octs - i, 1, 0)]))
        both_ways(jobs)

    def forward(slot, ff, o):
        return pltpu.make_async_remote_copy(
            src_ref=total.at[slot, rows_of(o), :], dst_ref=fwd.at[slot, rows_of(o), :],
            send_sem=gsend.at[slot, o], recv_sem=grecv.at[slot, o],
            device_id=dev(ff, p), device_id_type=MESH,
        )

    def settle(slot, target):
        def step(o, carry):
            here = valid(slot, o, p)

            @pl.when(here)
            def _():
                value = total[slot, rows_of(o), :]
                for hop in range(1, nz):
                    source = lax.rem(z + hop, nz)
                    z_copy(slot, o, z, source).wait_recv()
                    value = value + zin[slot, source, rows_of(o), :].astype(f32)
                total[slot, rows_of(o), :] = value
                if target is not None:
                    forward(slot, target, o).start()

            if target is None:
                @pl.when(jnp.logical_not(here))
                def _():
                    total[slot, rows_of(o), :] = jnp.zeros((oct_rows, LANES), f32)

            return carry

        lax.fori_loop(0, octs, step, 0)

    settle(XG, mate)
    settle(DG, f - 2)
    settle(OWN, None)

    def drain(slot):
        def step(i, carry):
            pp, o = i // octs, lax.rem(i, octs)
            zd = pp // CORES

            @pl.when(valid(slot, o, pp))
            def _():
                @pl.when(lax.rem(pp, CORES) != core)
                def _():
                    core_copy(slot, o, pp).wait_send()

                @pl.when(jnp.logical_and(lax.rem(pp, CORES) == core, z != zd))
                def _():
                    z_copy(slot, o, zd, z).wait_send()

            return carry

        lax.fori_loop(0, npan * octs, step, 0)

    for slot in (OWN, XG, DG):
        drain(slot)

    mate_gives = jnp.logical_or(odd == 0, f + 1 < nf)

    def take(slot, giver, comes):
        def step(o, carry):
            @pl.when(comes(o))
            def _():
                forward(slot, giver, o).wait_recv()
                total[OWN, rows_of(o), :] = total[OWN, rows_of(o), :] + fwd[slot, rows_of(o), :]

            return carry

        lax.fori_loop(0, octs, step, 0)

    def from_mate(o):
        t = o + p
        return jnp.logical_and(mate_gives, jnp.logical_and(t >= octs - 1, t <= 2 * octs - 1))

    def from_upper(o):
        t = o + p
        reach = jnp.logical_or(t >= 2 * octs - 1, jnp.logical_and(odd == 1, t >= octs - 1))
        return jnp.logical_and(has_u, reach)

    take(XG, mate, from_mate)
    take(DG, f - 2, from_upper)

    fin[...] = total[OWN]
    eye = lax.broadcasted_iota(jnp.int32, (freqs, freqs), 0) == lax.broadcasted_iota(
        jnp.int32, (freqs, freqs), 1
    )
    width = jnp.sum(
        jnp.where(eye, jnp.broadcast_to(bw_ref[...].astype(f32), (freqs, freqs)), 0.0), 1, keepdims=True
    )
    width = jnp.broadcast_to(width, (freqs, LANES))
    norm = jnp.float32(1.0 / math.sqrt(panels * npan))
    part = lax.broadcasted_iota(jnp.int32, (freqs, LANES), 1) // COMP
    for h in range(COMP // 8):
        values = [fin[pl.ds(h * 8 + a, freqs, stride=COMP), :] for a in range(8)]
        for bit in (1, 2, 4):
            upper = lax.rem(part // bit, 2) == 1
            fresh = list(values)
            for i in range(8):
                if i & bit:
                    continue
                j = i | bit
                fresh[i] = jnp.where(upper, pltpu.roll(values[j], COMP * bit, 1), values[i])
                fresh[j] = jnp.where(upper, values[j], pltpu.roll(values[i], LANES - COMP * bit, 1))
            values = fresh
        for k in range(8):
            offset = (p * 8 + k + 1).astype(f32)
            live = offset <= width
            start = (k * (COMP // 8) + h) * LANES
            out_ref[:, start:start + LANES] = jnp.where(live, values[k] * norm, 0.0)

    def close(o, carry):
        to_mate(o).wait_send()

        @pl.when(has_d)
        def _():
            to_lower(o).wait_send()

        @pl.when(has_u)
        def _():
            to_upper(o).wait_send()

        @pl.when(valid(XG, o, p))
        def _():
            forward(XG, mate, o).wait_send()

        @pl.when(valid(DG, o, p))
        def _():
            forward(DG, f - 2, o).wait_send()

        return carry

    lax.fori_loop(0, octs, close, 0)


def fused(nf, npan, fields, quad_index, band_width):
    freqs, comp, panels = fields.shape
    rows = freqs * comp
    nz = npan // CORES
    half = panels // 2
    octs = freqs // 8
    out_cols = REACH * freqs * comp * comp // npan
    bf16, f32 = jnp.bfloat16, jnp.float32
    dma = pltpu.SemaphoreType.DMA
    vmem = pl.BlockSpec(memory_space=pltpu.VMEM)
    return pl.pallas_call(
        functools.partial(kernel, nf, npan),
        out_shape=jax.ShapeDtypeStruct((freqs, out_cols), f32),
        in_specs=[pl.BlockSpec(memory_space=pl.ANY), vmem, vmem],
        out_specs=vmem,
        scratch_shapes=[
            pltpu.VMEM((rows, panels), bf16),
            pltpu.VMEM((rows, panels), bf16),
            pltpu.VMEM((rows, half), bf16),
            pltpu.VMEM((rows, half), bf16),
            pltpu.VMEM((rows, half), bf16),
            pltpu.VMEM((rows, half), bf16),
            pltpu.VMEM((rows, half), bf16),
            pltpu.VMEM((3, rows, (REACH + 1) * rows), f32),
            pltpu.VMEM((3, npan, rows, LANES), f32),
            pltpu.VMEM((3, npan, rows, LANES), bf16),
            pltpu.VMEM((3, nz, rows, LANES), bf16),
            pltpu.VMEM((3, nz, rows, LANES), bf16),
            pltpu.VMEM((3, nz, rows, LANES), bf16),
            pltpu.VMEM((3, rows, LANES), f32),
            pltpu.VMEM((3, rows, LANES), f32),
            pltpu.VMEM((rows, LANES), f32),
            dma,
            dma((3, octs)), dma((3, octs)),
            dma((3, nz, octs)), dma((3, nz, octs)),
            dma((3, nz, octs)), dma((3, nz, octs)),
            dma((3, octs)), dma((3, octs)),
        ],
        compiler_params=pltpu.CompilerParams(
            collective_id=0, has_side_effects=True, vmem_limit_bytes=58 * 1024 * 1024
        ),
    )(fields.reshape(rows, panels), quad_index.reshape(1, panels), band_width.reshape(1, freqs))


def local(nf, npan, fields, quad_index, band_width):
    freqs, comp, panels = fields.shape
    share = REACH * freqs * comp // npan
    fits = nf % 2 == 0 and npan % CORES == 0 and share == LANES and freqs % 8 == 0 and panels % (4 * LANES) == 0
    if not fits:
        return plain(fields, quad_index, band_width)
    return fused(nf, npan, fields, quad_index, band_width)


def solution(mesh):
    placed = (P("freq", None, "panel"), P("panel"), P("freq"))
    return jax.shard_map(
        functools.partial(local, mesh.shape["freq"], mesh.shape["panel"]),
        mesh=mesh, in_specs=placed, out_specs=P("freq", "panel"), check_vma=False,
    )
```

```python
import functools
import math

import jax
import jax.numpy as jnp
from jax import lax
from jax.experimental import pallas as pl
from jax.experimental.pallas import tpu as pltpu
from jax.sharding import PartitionSpec as P

COMP = 16
REACH = 2
LANES = 128
CORES = 2
MESH = pl.DeviceIdType.MESH

QUAD_TABLE = (0.2, 0.45, 0.8, 1.1, 1.6, 2.3)


def shifted(x, axis, by):
    devices = lax.axis_size(axis)
    pairs = [(i, i + by) for i in range(devices) if 0 <= i + by < devices]
    return lax.ppermute(x, axis, pairs)


def plain(fields, quad_index, band_width):
    freq_local = fields.shape[0]
    panel_local = fields.shape[2]
    band = REACH * freq_local
    table = jnp.asarray(QUAD_TABLE, jnp.float32)
    matches = quad_index[None, :] == jnp.arange(6, dtype=jnp.int32)[:, None]
    weight = jnp.sum(jnp.where(matches, table[:, None], jnp.float32(0.0)), 0)
    scaled = (fields.astype(jnp.float32) * weight).astype(jnp.bfloat16)
    own_rows = scaled.reshape(freq_local * COMP, panel_local)
    partners = [fields]
    for distance in range(1, REACH + 1):
        partners.append(shifted(fields, "freq", -distance))
    grams = []
    for partner in partners:
        grams.append(
            lax.dot_general(
                own_rows,
                partner.reshape(freq_local * COMP, panel_local),
                (((1,), (1,)), ((), ())),
                preferred_element_type=jnp.float32,
            )
        )
    stacked = jnp.concatenate(grams, 1).reshape(freq_local, COMP, (REACH + 1) * freq_local, COMP)

    def pick_band(block, row_index):
        return lax.dynamic_slice_in_dim(block, row_index + 1, band, 1)

    picked = jax.vmap(pick_band)(stacked, jnp.arange(freq_local, dtype=jnp.int32))
    picked = picked.transpose(0, 2, 1, 3)
    offsets = jnp.arange(band, dtype=jnp.int32) + 1
    live_mask = offsets[None, :] <= band_width[:, None]
    picked = jnp.where(live_mask[:, :, None, None], picked, jnp.float32(0.0))
    panels_total = panel_local * lax.axis_size("panel")
    terms = picked.reshape(freq_local, band * COMP * COMP) * jnp.float32(
        1.0 / math.sqrt(panels_total)
    )
    return lax.psum_scatter(terms, "panel", scatter_dimension=1, tiled=True)


OWN, XG, DG = 0, 1, 2


def kernel(
    nf, npan, f_hbm, q_ref, bw_ref, out_ref,
    own, scaled, xbuf, ubuf, dbuf, xs, ds, acc, keep, away, cxin, zout, zin, total, give, fwd, fin,
    local_sem, fsend, frecv, csend, crecv, zsend, zrecv, gsend, grecv,
):
    rows, panels = own.shape
    half = panels // 2
    block = rows
    freqs = rows // COMP
    oct_rows = 8 * COMP
    octs = rows // oct_rows
    nz = npan // CORES
    f32, bf16 = jnp.float32, jnp.bfloat16

    f = lax.axis_index("freq")
    p = lax.axis_index("panel")
    z, core = p // CORES, lax.rem(p, CORES)
    odd = lax.rem(f, 2)
    mate = f + 1 - 2 * odd
    has_u = f + 2 < nf
    has_d = f >= 2
    has_x = jnp.logical_or(odd == 1, has_u)
    partner = p + 1 - 2 * core

    def dev(ff, pp):
        return {"freq": ff, "panel": pp}

    load = pltpu.make_async_copy(f_hbm, own, local_sem)
    load.start()

    barrier = pltpu.get_barrier_semaphore()

    def greet(ff, pp):
        pl.semaphore_signal(barrier, inc=1, device_id=dev(ff, pp), device_id_type=MESH)

    greet(mate, p)
    greet(f, partner)
    for zd in range(nz):
        @pl.when(z != zd)
        def _(zd=zd):
            greet(f, zd * CORES + core)

    @pl.when(has_u)
    def _():
        greet(f + 2, p)

    @pl.when(has_d)
    def _():
        greet(f - 2, p)

    count = 1 + nz + jnp.where(has_u, 1, 0) + jnp.where(has_d, 1, 0)
    pl.semaphore_wait(barrier, count)

    def half_at(which):
        return pl.ds(pl.multiple_of(which * half, LANES), half)

    def rows_of(o, n=1):
        return pl.ds(pl.multiple_of(o * oct_rows, oct_rows), n * oct_rows)

    def field_copy(which, dst, slot, ff, o):
        return pltpu.make_async_remote_copy(
            src_ref=f_hbm.at[rows_of(o), half_at(which)], dst_ref=dst.at[rows_of(o), :],
            send_sem=fsend.at[slot, o], recv_sem=frecv.at[slot, o],
            device_id=dev(ff, p), device_id_type=MESH,
        )

    def to_mate(o):
        return field_copy(1 - odd, xbuf, 0, mate, o)

    def to_lower(o):
        return field_copy(0, ubuf, 1, f - 2, o)

    def to_upper(o):
        return field_copy(1, dbuf, 2, f + 2, o)

    for o in range(octs):
        to_mate(octs - 1 - o).start()

        @pl.when(has_d)
        def _(o=o):
            to_lower(o).start()

        @pl.when(has_u)
        def _(o=o):
            to_upper(octs - 1 - o).start()

    def weight_at(where):
        index = q_ref[:, where]
        w = jnp.zeros(index.shape, f32)
        for value, entry in enumerate(QUAD_TABLE):
            w = jnp.where(index == value, jnp.float32(entry), w)
        return w

    def scale(src, dst, where, o, n):
        w = weight_at(where)

        def step(i, carry):
            at = pl.ds(pl.multiple_of(o * oct_rows + i * 32, 32), 32)
            dst[at, :] = (src[at, :].astype(f32) * w).astype(bf16)
            return carry

        lax.fori_loop(0, n * oct_rows // 32, step, 0)

    def gram(left, left_at, lo, n, right, right_at, ro, m, slot, rel):
        tall = 2 if n % 2 == 0 else 1
        first_col = rel * block + ro * oct_rows

        def step(i, carry):
            at = rows_of(lo + i * tall, tall)
            acc[slot, at, first_col:first_col + m * oct_rows] = lax.dot_general(
                left[at, left_at], right[ro * oct_rows:(ro + m) * oct_rows, right_at],
                (((1,), (1,)), ((), ())), preferred_element_type=f32,
            )
            return carry

        if n == tall:
            step(0, 0)
        else:
            lax.fori_loop(0, n // tall, step, 0)

    def clear(slot, tile):
        acc[slot, :, tile * LANES:(tile + 1) * LANES] = jnp.zeros((rows, LANES), f32)

    clear(XG, octs - 1)
    clear(XG, 2 * octs)
    clear(DG, octs - 1)

    @pl.when(odd == 0)
    def _():
        clear(DG, 2 * octs - 1)

    @pl.when(odd == 1)
    def _():
        clear(OWN, octs)
        clear(OWN, 2 * octs - 1)

    @pl.when(jnp.logical_not(has_u))
    def _():
        clear(OWN, 2 * octs)

    def valid(slot, o, pp):
        t = o + pp
        low, high = t >= octs - 1, t <= 2 * octs - 1
        if slot == OWN:
            return jnp.logical_or(
                t <= octs - 1,
                jnp.logical_or(
                    jnp.logical_and(odd == 0, high),
                    jnp.logical_and(has_u, t >= 2 * octs - 1),
                ),
            )
        if slot == XG:
            return jnp.logical_and(has_x, jnp.logical_and(low, high))
        upper = jnp.logical_or(t >= 2 * octs - 1, jnp.logical_and(odd == 1, low))
        return jnp.logical_and(has_d, upper)

    def core_copy(slot, o, pp):
        zd = pp // CORES
        return pltpu.make_async_remote_copy(
            src_ref=away.at[slot, pp, rows_of(o), :], dst_ref=cxin.at[slot, zd, rows_of(o), :],
            send_sem=csend.at[slot, zd, o], recv_sem=crecv.at[slot, zd, o],
            device_id=dev(f, partner), device_id_type=MESH,
        )

    def z_copy(slot, o, zd, source):
        return pltpu.make_async_remote_copy(
            src_ref=zout.at[slot, zd, rows_of(o), :], dst_ref=zin.at[slot, source, rows_of(o), :],
            send_sem=zsend.at[slot, zd, o], recv_sem=zrecv.at[slot, source, o],
            device_id=dev(f, zd * CORES + core), device_id_type=MESH,
        )

    def walk(act, slot, o, t, n, do, dt):
        def step(i, carry):
            oo, tt = o + i * do, t + i * dt
            act(slot, oo, tt - oo, tt)
            return carry

        if n > 0:
            lax.fori_loop(0, n, step, 0)

    def make(slot, o, pp, t):
        lane = pl.multiple_of(t * LANES, LANES)
        for c in range(8):
            at = pl.ds(pl.multiple_of(o * oct_rows + c * COMP, COMP), COMP)
            if c == 7:
                value = acc[slot, at, pl.ds(pl.multiple_of(lane + LANES, LANES), LANES)]
            else:
                pair = acc[slot, at, pl.ds(lane, 2 * LANES)]
                value = pltpu.roll(pair, 2 * LANES - COMP * (c + 1), 1)[:, :LANES]
            keep[slot, pp, at, :] = value
            away[slot, pp, at, :] = value.astype(bf16)

        @pl.when(lax.rem(pp, CORES) != core)
        def _():
            core_copy(slot, o, pp).start()

    def join(slot, o, pp, t):
        @pl.when(lax.rem(pp, CORES) == core)
        def _():
            zd = pp // CORES
            core_copy(slot, o, pp).wait_recv()
            both = keep[slot, pp, rows_of(o), :] + cxin[slot, zd, rows_of(o), :].astype(f32)

            @pl.when(z == zd)
            def _():
                total[slot, rows_of(o), :] = both

            @pl.when(z != zd)
            def _():
                zout[slot, zd, rows_of(o), :] = both.astype(bf16)
                z_copy(slot, o, zd, z).start()

    def both_ways(jobs):
        for act in (make, join):
            for job in jobs:
                if len(job) == 2:
                    @pl.when(job[0])
                    def _(job=job, act=act):
                        for inner in job[1]:
                            walk(act, *inner)
                else:
                    walk(act, *job)

    load.wait()
    everything = pl.ds(0, panels)
    first = pl.ds(0, half)
    second = pl.ds(half, half)
    even_now, odd_now = odd == 0, odd == 1
    scale(own, scaled, everything, 0, octs)
    gram(scaled, everything, 0, octs, own, everything, 0, octs, OWN, 0)
    jobs = [(OWN, 0, t, t + 1, 1, 0) for t in range(octs - 1)]
    jobs.append((odd_now, [(OWN, 0, octs - 1, octs, 1, 0)]))
    both_ways(jobs)

    for i in range(octs):
        x = octs - 1 - i
        last = i == octs - 1
        to_mate(x).wait_recv()
        scale(xbuf, xs, half_at(odd), x, 1)
        jobs = []

        @pl.when(odd_now)
        def _(x=x):
            gram(xs, first, x, 1, own, second, 0, octs, XG, 1)

        jobs.append((odd_now, [(XG, x, octs - 1, octs + 1, 0, 1)]))

        @pl.when(even_now)
        def _(x=x):
            gram(scaled, first, 0, octs, xbuf, first, x, 1, OWN, 1)

        @pl.when(has_u)
        def _(i=i):
            to_lower(i).wait_recv()
            gram(scaled, first, i, octs - i, ubuf, first, i, 1, OWN, 2)

        @pl.when(jnp.logical_and(has_u, even_now))
        def _(i=i, x=x):
            gram(xs, first, x, 1, ubuf, first, 0, i + 1, XG, 1)
            if i:
                gram(xs, first, x + 1, i, ubuf, first, i, 1, XG, 1)

        mixed = [(XG, x, octs - 1, i + 1 + last, 0, 1), (XG, x + 1, octs - 1 + i, i, 1, 0)]
        if last:
            mixed.append((XG, x + 1, 2 * octs - 1, i, 1, 0))
        jobs.append((jnp.logical_and(has_u, even_now), mixed))

        @pl.when(has_d)
        def _(x=x):
            to_upper(x).wait_recv()
            scale(dbuf, ds, second, x, 1)
            gram(ds, first, x, 1, own, second, 0, x + 1, DG, 2)

        @pl.when(jnp.logical_and(has_d, odd_now))
        def _(i=i, x=x):
            gram(ds, first, x, 1, xbuf, first, x, i + 1, DG, 1)
            if i:
                gram(ds, first, x + 1, i, xbuf, first, x, 1, DG, 1)

        mixed = [
            (DG, x, octs + x - last, i + 1 + last, 0, 1),
            (DG, x + 1, octs + x, i, 1, 0),
            (DG, x, 2 * octs, x, 0, 1),
        ]
        if last:
            mixed.append((DG, x + 1, octs - 1, i, 1, 0))
        jobs.append((jnp.logical_and(has_d, odd_now), mixed))
        jobs.append((jnp.logical_and(has_d, even_now), [(DG, x, 2 * octs - 1, x + 1, 0, 1)]))
        own_even = [(OWN, 0, octs + x, octs, 1, 0)]
        if last:
            own_even.append((OWN, 0, octs - 1, octs, 1, 0))
        jobs.append((even_now, own_even))
        if i == 0:
            jobs.append((jnp.logical_and(has_u, odd_now), [(OWN, 0, 2 * octs - 1, octs, 1, 0)]))
        else:
            jobs.append((has_u, [(OWN, i, 2 * octs - 1 + i, octs - i, 1, 0)]))
        both_ways(jobs)

    def forward(slot, ff, o):
        return pltpu.make_async_remote_copy(
            src_ref=give.at[slot, rows_of(o), :], dst_ref=fwd.at[slot, rows_of(o), :],
            send_sem=gsend.at[slot, o], recv_sem=grecv.at[slot, o],
            device_id=dev(ff, p), device_id_type=MESH,
        )

    def settle(slot, target):
        def step(o, carry):
            here = valid(slot, o, p)

            @pl.when(here)
            def _():
                value = total[slot, rows_of(o), :]
                for hop in range(1, nz):
                    source = lax.rem(z + hop, nz)
                    z_copy(slot, o, z, source).wait_recv()
                    value = value + zin[slot, source, rows_of(o), :].astype(f32)
                total[slot, rows_of(o), :] = value
                if target is not None:
                    give[slot, rows_of(o), :] = value.astype(bf16)
                    forward(slot, target, o).start()

            if target is None:
                @pl.when(jnp.logical_not(here))
                def _():
                    total[slot, rows_of(o), :] = jnp.zeros((oct_rows, LANES), f32)

            return carry

        lax.fori_loop(0, octs, step, 0)

    settle(XG, mate)
    settle(DG, f - 2)
    settle(OWN, None)

    def drain(slot):
        def step(i, carry):
            pp, o = i // octs, lax.rem(i, octs)
            zd = pp // CORES

            @pl.when(valid(slot, o, pp))
            def _():
                @pl.when(lax.rem(pp, CORES) != core)
                def _():
                    core_copy(slot, o, pp).wait_send()

                @pl.when(jnp.logical_and(lax.rem(pp, CORES) == core, z != zd))
                def _():
                    z_copy(slot, o, zd, z).wait_send()

            return carry

        lax.fori_loop(0, npan * octs, step, 0)

    for slot in (OWN, XG, DG):
        drain(slot)

    mate_gives = jnp.logical_or(odd == 0, f + 1 < nf)

    def take(slot, giver, comes):
        def step(o, carry):
            @pl.when(comes(o))
            def _():
                forward(slot, giver, o).wait_recv()
                total[OWN, rows_of(o), :] = total[OWN, rows_of(o), :] + fwd[slot, rows_of(o), :].astype(f32)

            return carry

        lax.fori_loop(0, octs, step, 0)

    def from_mate(o):
        t = o + p
        return jnp.logical_and(mate_gives, jnp.logical_and(t >= octs - 1, t <= 2 * octs - 1))

    def from_upper(o):
        t = o + p
        reach = jnp.logical_or(t >= 2 * octs - 1, jnp.logical_and(odd == 1, t >= octs - 1))
        return jnp.logical_and(has_u, reach)

    take(XG, mate, from_mate)
    take(DG, f - 2, from_upper)

    fin[...] = total[OWN]
    eye = lax.broadcasted_iota(jnp.int32, (freqs, freqs), 0) == lax.broadcasted_iota(
        jnp.int32, (freqs, freqs), 1
    )
    width = jnp.sum(
        jnp.where(eye, jnp.broadcast_to(bw_ref[...].astype(f32), (freqs, freqs)), 0.0), 1, keepdims=True
    )
    width = jnp.broadcast_to(width, (freqs, LANES))
    norm = jnp.float32(1.0 / math.sqrt(panels * npan))
    part = lax.broadcasted_iota(jnp.int32, (freqs, LANES), 1) // COMP
    for h in range(COMP // 8):
        values = [fin[pl.ds(h * 8 + a, freqs, stride=COMP), :] for a in range(8)]
        for bit in (1, 2, 4):
            upper = lax.rem(part // bit, 2) == 1
            fresh = list(values)
            for i in range(8):
                if i & bit:
                    continue
                j = i | bit
                fresh[i] = jnp.where(upper, pltpu.roll(values[j], COMP * bit, 1), values[i])
                fresh[j] = jnp.where(upper, values[j], pltpu.roll(values[i], LANES - COMP * bit, 1))
            values = fresh
        for k in range(8):
            offset = (p * 8 + k + 1).astype(f32)
            live = offset <= width
            start = (k * (COMP // 8) + h) * LANES
            out_ref[:, start:start + LANES] = jnp.where(live, values[k] * norm, 0.0)

    def close(o, carry):
        to_mate(o).wait_send()

        @pl.when(has_d)
        def _():
            to_lower(o).wait_send()

        @pl.when(has_u)
        def _():
            to_upper(o).wait_send()

        @pl.when(valid(XG, o, p))
        def _():
            forward(XG, mate, o).wait_send()

        @pl.when(valid(DG, o, p))
        def _():
            forward(DG, f - 2, o).wait_send()

        return carry

    lax.fori_loop(0, octs, close, 0)


def fused(nf, npan, fields, quad_index, band_width):
    freqs, comp, panels = fields.shape
    rows = freqs * comp
    nz = npan // CORES
    half = panels // 2
    octs = freqs // 8
    out_cols = REACH * freqs * comp * comp // npan
    bf16, f32 = jnp.bfloat16, jnp.float32
    dma = pltpu.SemaphoreType.DMA
    vmem = pl.BlockSpec(memory_space=pltpu.VMEM)
    return pl.pallas_call(
        functools.partial(kernel, nf, npan),
        out_shape=jax.ShapeDtypeStruct((freqs, out_cols), f32),
        in_specs=[pl.BlockSpec(memory_space=pl.ANY), vmem, vmem],
        out_specs=vmem,
        scratch_shapes=[
            pltpu.VMEM((rows, panels), bf16),
            pltpu.VMEM((rows, panels), bf16),
            pltpu.VMEM((rows, half), bf16),
            pltpu.VMEM((rows, half), bf16),
            pltpu.VMEM((rows, half), bf16),
            pltpu.VMEM((rows, half), bf16),
            pltpu.VMEM((rows, half), bf16),
            pltpu.VMEM((3, rows, (REACH + 1) * rows), f32),
            pltpu.VMEM((3, npan, rows, LANES), f32),
            pltpu.VMEM((3, npan, rows, LANES), bf16),
            pltpu.VMEM((3, nz, rows, LANES), bf16),
            pltpu.VMEM((3, nz, rows, LANES), bf16),
            pltpu.VMEM((3, nz, rows, LANES), bf16),
            pltpu.VMEM((3, rows, LANES), f32),
            pltpu.VMEM((3, rows, LANES), bf16),
            pltpu.VMEM((3, rows, LANES), bf16),
            pltpu.VMEM((rows, LANES), f32),
            dma,
            dma((3, octs)), dma((3, octs)),
            dma((3, nz, octs)), dma((3, nz, octs)),
            dma((3, nz, octs)), dma((3, nz, octs)),
            dma((3, octs)), dma((3, octs)),
        ],
        compiler_params=pltpu.CompilerParams(
            collective_id=0, has_side_effects=True, vmem_limit_bytes=58 * 1024 * 1024
        ),
    )(fields.reshape(rows, panels), quad_index.reshape(1, panels), band_width.reshape(1, freqs))


def local(nf, npan, fields, quad_index, band_width):
    freqs, comp, panels = fields.shape
    share = REACH * freqs * comp // npan
    fits = nf % 2 == 0 and npan % CORES == 0 and share == LANES and freqs % 8 == 0 and panels % (4 * LANES) == 0
    if not fits:
        return plain(fields, quad_index, band_width)
    return fused(nf, npan, fields, quad_index, band_width)


def solution(mesh):
    placed = (P("freq", None, "panel"), P("panel"), P("freq"))
    return jax.shard_map(
        functools.partial(local, mesh.shape["freq"], mesh.shape["panel"]),
        mesh=mesh, in_specs=placed, out_specs=P("freq", "panel"), check_vma=False,
    )
```
